32 devices in a mesh: groups: 2 (over y), expert: 4 (over z), token: 4 (over x, core).
Axes of the slice: x: 2, y: 2, z: 4, core: 2. Of those that a mesh axis runs over, the one named last changes fastest.
Arguments:
- tokens: bfloat16 [512, 2048], P(('groups', 'expert'), 'token'), parts along dimension 0, may hold values from -6 to 6
- expert_ids: int32 [512, 8], P(('groups', 'expert')), parts along dimension 0, may hold values from 0 to 15, all different within a row; in each aligned block of 64 rows (0 to 63, 64 to 127, ...) at most 64 rows name the same one
- route_weights: float32 [512, 8], P(('groups', 'expert')), parts along dimension 0, may hold values from 0.1 to 0.4
- w_gate_up: bfloat16 [16, 2048, 1536], P('expert', 'token'), may hold values from -0.125 to 0.125
- w_down: bfloat16 [16, 768, 2048], P('expert', None, 'token'), may hold values from -0.21875 to 0.21875
Outputs:
- combined: bfloat16 [512, 2048], P(('groups', 'expert'), 'token'), parts along dimension 0
The draws below stay inside these ranges and needn't reach their ends.
There are 2 independent parts, one for each index of `groups`. The reference program is written for one: setup_inputs(seed, part) draws one part's arguments, and reference() takes and returns one part's arrays. A program takes and returns all parts, laid end to end along the dimension named above; an argument that names none is the same for every part. Nothing has to cross between parts.
Inputs may be any that keep to these rules, and one draw needn't show every extreme that they name: `expert_ids`: each row names 8 different experts. In each aligned block of 64 rows no expert is named by more than 64 rows, a bound that some block reaches.
All inputs are finite; a program needn't handle non-finite values.
Results may differ from the reference program's by a relative error of at most 0.02.
Values may be sent and summed in bfloat16 or wider, within the bound.
A program may use at most 64 MiB of HBM per device.

```python
import math
import jax
import jax.numpy as jnp
import numpy as np
from jax import lax

D = 2048
FF = 768
TOP = 8
TOK_DEV = 64
EXPERTS = 16
TOKENS = 256
CAP = 64
N_EXPERT = 4
N_TOKEN = 4


def levels(stream_key, shape, shards, least, largest):
    gain = 1.0
    for dim, parts in shards:
        heights = jax.random.uniform(jax.random.fold_in(jax.random.fold_in(stream_key, 6), dim), (parts,), jnp.float32, least / len(shards), largest / len(shards))
        gain = gain * jnp.repeat(jnp.exp(heights), shape[dim] // parts).reshape((-1,) + (1,) * (len(shape) - 1 - dim))
    return gain


def deal_out(rng, own, number, rows, number_of, top, reach, slope):
    sequence = jax.random.permutation(rng, number_of)
    packed, usual = shares(number_of, rows * top, reach, slope, True), shares(number_of, rows * top, reach, slope, False)
    places = jnp.arange(number_of)

    def named(sizes, offset_by):
        used = int((sizes > 0).sum())
        fixed = max(1, used // 4)
        passed = fixed + (places - fixed + offset_by * (used - fixed)) % max(1, number_of - fixed)
        return jnp.zeros((number_of,), jnp.int32).at[sequence[jnp.where(places < fixed, places, passed)]].set(jnp.asarray(sizes, jnp.int32))

    sizes = jnp.where(number % 4 == 0, named(packed, number // 4), named(usual, number - number // 4 - 1))
    mixed = jax.random.permutation(jax.random.fold_in(own, 3), number_of)
    source_of, sink = mixed[0:number_of // 2 * 2:2], mixed[1:number_of // 2 * 2:2]
    slack = jnp.minimum(sizes[source_of] - 1, reach - sizes[sink]) // 2
    slack = jnp.where((source_of == sequence[0]) | (sink == sequence[0]) | (sizes[sink] == 0), 0, jnp.maximum(slack, 0))
    passed = jax.random.randint(jax.random.fold_in(own, 4), (number_of // 2,), 0, 1 << 20) % (slack + 1)
    sizes = sizes.at[source_of].add(-passed).at[sink].add(passed)
    labels = jnp.searchsorted(jnp.cumsum(sizes), jnp.arange(rows * top), side="right").astype(jnp.int32)
    listing = labels.reshape(top, rows).T
    listing = listing[jax.random.permutation(jax.random.fold_in(own, 1), rows)]
    offset_by = jax.random.randint(jax.random.fold_in(own, 2), (rows, 1), 0, top)
    return jnp.take_along_axis(listing, (jnp.arange(top)[None, :] + offset_by) % top, axis=1)


def shares(count, total, most, slope, full):
    portions = [(1 << 20) // math.isqrt(rank ** slope) + 1 for rank in range(1, count + 1)]
    largest = most if full else min(most, max(-(-total // count), total * portions[0] // sum(portions)))
    least = 1 if total - largest >= count - 1 else 0
    counts, spare = [largest] + [least] * (count - 1), total - largest - least * (count - 1)
    while spare > 0:
        candidates = [i for i in range(1, count) if counts[i] < largest] or [i for i in range(1, count) if counts[i] < most]
        mass, budget = sum([portions[i] for i in candidates]), spare
        for i in candidates:
            more = min(most - counts[i], max(1, budget * portions[i] // mass), spare)
            counts[i] = counts[i] + more
            spare = spare - more
    return np.array(counts)


def centred(own_key, extent, scale, limit, split=(), kind=jnp.bfloat16):
    array = jax.random.normal(own_key, extent, jnp.float32) * scale
    if len(split) > 0:
        array = levels(own_key, extent, split, -0.22, 0.18) * array
    return jnp.clip(array, min=-limit, max=limit).astype(kind)


def setup_inputs(seed: int = 0, part: int = 0) -> dict:
    key_list = jax.random.split(jax.random.key(seed), 6)
    own_keys = jax.random.split(jax.random.fold_in(key_list[5], part), 6)
    tokens = centred(own_keys[0], (TOKENS, D), 1.0, 6.0, ((0, 4), (1, 4)))
    expert_ids_keys = jax.random.split(jax.random.fold_in(own_keys[1], 1), TOKENS // TOK_DEV)
    expert_ids_turns = jax.random.permutation(jax.random.fold_in(own_keys[1], 3), TOKENS // TOK_DEV)
    expert_ids = jax.vmap(lambda own, number: deal_out(jax.random.fold_in(own_keys[1], 2), own, number, TOK_DEV, EXPERTS, TOP, CAP, 2))(expert_ids_keys, expert_ids_turns).reshape((TOKENS, TOP))
    route_weights = jnp.clip(0.1 + 0.3 * jax.random.uniform(own_keys[2], (TOKENS, TOP), jnp.float32) ** levels(own_keys[2], (TOKENS, TOP), ((0, 4),), -0.2, 0.2), 0.1, 0.4)
    w_gate_up = centred(key_list[3], (EXPERTS, D, 2 * FF), D ** -0.5, 0.125, ((0, 4), (1, 4)))
    w_down = centred(key_list[4], (EXPERTS, FF, D), FF ** -0.5, 0.21875, ((0, 4), (2, 4)))
    return {"tokens": tokens, "expert_ids": expert_ids, "route_weights": route_weights, "w_gate_up": w_gate_up, "w_down": w_down}


def reference(tokens, expert_ids, route_weights, w_gate_up, w_down):
    slot_total = N_EXPERT * CAP
    flat_ids = expert_ids.reshape(-1)
    onehot = (flat_ids[:, None] == jnp.arange(EXPERTS, dtype=jnp.int32)[None, :]).astype(jnp.int32)
    rank_of = jnp.sum((jnp.cumsum(onehot, axis=0) - 1) * onehot, axis=1).astype(jnp.int32)
    position = (flat_ids * slot_total + rank_of).astype(jnp.int32)
    token_of = (jnp.arange(flat_ids.shape[0], dtype=jnp.int32) // TOP).astype(jnp.int32)
    slot_table = jnp.full((EXPERTS * slot_total,), TOKENS, jnp.int32).at[position].set(token_of)
    slot_table = slot_table.reshape(EXPERTS, slot_total)
    padded = jnp.concatenate([tokens, jnp.zeros((1, D), tokens.dtype)], axis=0)
    block_cols = D // N_TOKEN

    def one_expert(operand):
        rows_of, gate_up_w, down_w = operand
        row_block = jnp.take(padded, rows_of, axis=0)
        split_in = row_block.reshape(slot_total, N_TOKEN, block_cols).astype(jnp.float32)
        split_w = gate_up_w.reshape(N_TOKEN, block_cols, 2 * FF).astype(jnp.float32)
        partial_j = jnp.einsum("rjd,jdf->jrf", split_in, split_w).astype(jnp.bfloat16)
        gate_up = jnp.sum(partial_j.astype(jnp.float32), axis=0)
        hidden = (jax.nn.silu(gate_up[:, :FF]) * gate_up[:, FF:]).astype(jnp.bfloat16)
        return jnp.dot(hidden, down_w, preferred_element_type=jnp.float32).astype(jnp.bfloat16)

    outputs = lax.map(one_expert, (slot_table, w_gate_up, w_down))
    picked = jnp.take(outputs.reshape(EXPERTS * slot_total, D), position, axis=0).reshape(TOKENS, TOP, D)
    combined = jnp.sum(route_weights[:, :, None] * picked.astype(jnp.float32), axis=1)
    return combined.astype(jnp.bfloat16)
```

```python
import functools

import jax
import jax.numpy as jnp
from jax import lax
from jax.experimental import pallas as pl
from jax.experimental.pallas import tpu as pltpu
from jax.sharding import PartitionSpec as P

MESH = pl.DeviceIdType.MESH


def rank_slots(flat_ids):
    place = jnp.arange(flat_ids.shape[0], dtype=jnp.int32)
    earlier = (flat_ids[:, None] == flat_ids[None, :]) & (place[None, :] < place[:, None])
    return jnp.sum(earlier.astype(jnp.int32), axis=1)


def gate_up_terms(inputs, w_gate_up):
    return jnp.einsum("erd,edf->ref", inputs, w_gate_up, preferred_element_type=jnp.float32)


def expert_block(inputs, gate_up_w, down_w):
    hidden_units = gate_up_w.shape[2] // 2
    summed = lax.psum_scatter(
        gate_up_terms(inputs, gate_up_w).astype(jnp.bfloat16),
        "token",
        scatter_dimension=0,
        tiled=True,
    ).astype(jnp.float32)
    hidden = (jax.nn.silu(summed[..., :hidden_units]) * summed[..., hidden_units:]).astype(
        jnp.bfloat16
    )
    produced = jnp.einsum(
        "reh,ehd->erd",
        lax.all_gather(hidden, "token", axis=0, tiled=True),
        down_w,
        preferred_element_type=jnp.float32,
    )
    return produced.astype(jnp.bfloat16)


def slot_device(tokens, expert_ids, route_weights, w_gate_up, w_down):
    tok_dev, feature_cols = tokens.shape
    top_k = expert_ids.shape[1]
    local_experts = w_gate_up.shape[0]
    n_expert = lax.axis_size("expert")
    experts = local_experts * n_expert
    capacity = max(2, min(tok_dev, tok_dev * top_k * 5 // (2 * experts)))
    slot_count = n_expert * capacity
    flat_ids = expert_ids.reshape(-1)
    rank_of = rank_slots(flat_ids)
    position = (
        flat_ids % local_experts * slot_count + flat_ids // local_experts * capacity + rank_of
    )
    token_of = jnp.arange(flat_ids.shape[0], dtype=jnp.int32) // top_k
    slot_table = (
        jnp.full((local_experts * slot_count,), tok_dev, jnp.int32).at[position].set(token_of)
    )
    padded = jnp.concatenate([tokens, jnp.zeros((1, feature_cols), tokens.dtype)], axis=0)
    outgoing = jnp.take(padded, slot_table, axis=0).reshape(
        local_experts, n_expert, capacity, feature_cols
    )
    arrived = lax.all_to_all(outgoing, "expert", split_axis=1, concat_axis=1, tiled=True)
    inputs = arrived.reshape(local_experts, slot_count, feature_cols)
    expert_out = expert_block(inputs, w_gate_up, w_down)
    returned = lax.all_to_all(
        expert_out.reshape(local_experts, n_expert, capacity, feature_cols),
        "expert",
        split_axis=1,
        concat_axis=1,
        tiled=True,
    )
    picked = jnp.take(
        returned.reshape(local_experts * slot_count, feature_cols), position, axis=0
    ).reshape(tok_dev, top_k, feature_cols)
    combined = jnp.sum(route_weights[:, :, None] * picked.astype(jnp.float32), axis=1)
    return combined.astype(jnp.bfloat16)


def flip(index, bits):
    out, bit = index, 1
    while bit <= bits:
        if bits & bit:
            out = out + bit * (1 - 2 * ((index // bit) % 2))
        bit *= 2
    return out


def dense_kernel(
    chunks,
    tokens_ref,
    ids_hbm,
    weights_hbm,
    wg_hbm,
    wd_hbm,
    out_ref,
    wg,
    wd,
    ids_ref,
    weights_ref,
    tok,
    row_out,
    row_in,
    far_out,
    far_in,
    sum_out,
    sum_in,
    near_out,
    near_in,
    part,
    own,
    hid,
    back_out,
    back_in,
    total,
    load_sem,
    wg_sem,
    wd_sem,
    tok_s,
    tok_r,
    row_s,
    row_r,
    far_s,
    far_r,
    sum_s,
    sum_r,
    near_s,
    near_r,
    hid_s,
    hid_r,
    back_s,
    back_r,
):
    z = lax.axis_index("expert")
    t = lax.axis_index("token")
    rows = tokens_ref.shape[0]
    half = own.shape[2] // 2
    local = wg.shape[0]
    f32, bf16 = jnp.float32, jnp.bfloat16
    mate, across = {"token": flip(t, 1)}, {"token": flip(t, 2)}
    others = []
    for k, _, _ in chunks:
        if k and k not in others:
            others.append(k)

    barrier = pltpu.get_barrier_semaphore()
    partners = [mate, across] + [{"expert": flip(z, k)} for k in others]
    for partner in reversed(partners):
        pl.semaphore_signal(barrier, inc=1, device_id=partner, device_id_type=MESH)

    loads = [
        pltpu.make_async_copy(tokens_ref, tok.at[0], load_sem.at[0]),
        pltpu.make_async_copy(ids_hbm, ids_ref, load_sem.at[1]),
        pltpu.make_async_copy(weights_hbm, weights_ref, load_sem.at[2]),
    ]
    wg_copies, wd_copies = {}, {}
    for j in (3, 2, 1, 0):
        wg_copies[j] = pltpu.make_async_copy(wg_hbm.at[flip(t, j)], wg.at[j], wg_sem.at[j])
    for load in loads:
        load.start()
    for j in (3, 2):
        wg_copies[j].start()
    for load in loads:
        load.wait()

    for k in [0] + others:
        expert = flip(z, k) * local + t
        row = jnp.sum(
            jnp.where(ids_ref[...] == expert, weights_ref[...], 0.0), axis=0, keepdims=True
        )
        row_out[k] = jnp.broadcast_to(row, row_out.shape[1:])

    pending = []

    def send(src, dst, s_sem, r_sem, device):
        copy = pltpu.make_async_remote_copy(
            src_ref=src,
            dst_ref=dst,
            send_sem=s_sem,
            recv_sem=r_sem,
            device_id=device,
            device_id_type=MESH,
        )
        copy.start()
        pending.append(copy)
        return copy

    tok_c, row_c, far_c, sum_c, near_c, back_c = {}, {}, {}, {}, {}, {}
    hid_c = {}

    def terms(c, j):
        k, start, size = chunks[c]
        return jnp.dot(tok[k, pl.ds(start, size), :], wg[j], preferred_element_type=f32)

    def piece(c):
        k, start, size = chunks[c]
        return (k, pl.ds(start, size))

    def stage_a(c):
        k = chunks[c][0]
        here = piece(c)
        if k and chunks[c][1] == 0:
            tok_c[k].wait_recv()
        if c == 0:
            pl.semaphore_wait(barrier, len(partners))
            for o in others:
                there = {"expert": flip(z, o)}
                tok_c[o] = send(tokens_ref, tok.at[o], tok_s.at[o], tok_r.at[o], there)
            for j in (1, 0):
                wg_copies[j].start()
            wg_copies[3].wait()
        far_out[here] = terms(c, 3).astype(bf16)
        far_c[c] = send(far_out.at[here], far_in.at[here], far_s.at[c], far_r.at[c], mate)
        if c == 0:
            for j in range(local):
                wd_copies[j] = pltpu.make_async_copy(
                    wd_hbm.at[flip(t, j)], wd.at[j], wd_sem.at[j]
                )
                wd_copies[j].start()
            wg_copies[2].wait()
        part[here] = terms(c, 2)
        if c == 0:
            far_c[c].wait_recv()
            sum_out[here] = (part[here] + far_in[here].astype(f32)).astype(bf16)
            sum_c[c] = send(sum_out.at[here], sum_in.at[here], sum_s.at[c], sum_r.at[c], across)
            for o in others:
                there = {"expert": flip(z, o)}
                row_c[o] = send(row_out.at[o], row_in.at[o], row_s.at[o], row_r.at[o], there)
            wg_copies[1].wait()
        near_out[here] = terms(c, 1).astype(bf16)
        near_c[c] = send(near_out.at[here], near_in.at[here], near_s.at[c], near_r.at[c], mate)
        if c == 0:
            wg_copies[0].wait()
            own[here] = terms(c, 0)
            return
        far_c[c].wait_recv()
        sum_out[here] = (part[here] + far_in[here].astype(f32)).astype(bf16)
        sum_c[c] = send(sum_out.at[here], sum_in.at[here], sum_s.at[c], sum_r.at[c], across)
        own[here] = terms(c, 0)

    def stage_b(c):
        k, start, size = chunks[c]
        here = piece(c)
        near_c[c].wait_recv()
        if k and start == 0:
            row_c[k].wait_recv()
        row = row_in[k, :1, :] if k else row_out[k, :1, :]
        eye = start + lax.broadcasted_iota(
            jnp.int32, (size, rows), 0
        ) == lax.broadcasted_iota(jnp.int32, (size, rows), 1)
        column = jnp.sum(jnp.where(eye, row, 0.0), axis=1, keepdims=True)
        sum_c[c].wait_recv()
        gate_up = own[here] + near_in[here].astype(f32) + sum_in[here].astype(f32)
        gate, up = gate_up[:, :half], gate_up[:, half:]
        at = pl.ds(start, size)
        hid[k, 0, at] = (gate / (1.0 + jnp.exp(-gate)) * up * column).astype(bf16)
        for j, device in ((2, across), (1, mate)):
            hid_c[c, j] = send(
                hid.at[k, 0, at], hid.at[k, j, at], hid_s.at[c, j], hid_r.at[c, j], device
            )

    def stage_f(c):
        k, start, size = chunks[c]
        at = pl.ds(start, size)
        hid_c[c, 2].wait_recv()
        hid_c[c, 3] = send(
            hid.at[k, 2, at], hid.at[k, 3, at], hid_s.at[c, 3], hid_r.at[c, 3], mate
        )

    def stage_c(c):
        k, start, size = chunks[c]
        at = pl.ds(start, size)
        if c == 0:
            for j in range(local):
                wd_copies[j].wait()
        acc = jnp.dot(hid[k, 0, at], wd[0], preferred_element_type=f32)
        hid_c[c, 1].wait_recv()
        acc = acc + jnp.dot(hid[k, 1, at], wd[1], preferred_element_type=f32)
        acc = acc + jnp.dot(hid[k, 2, at], wd[2], preferred_element_type=f32)
        hid_c[c, 3].wait_recv()
        acc = acc + jnp.dot(hid[k, 3, at], wd[3], preferred_element_type=f32)
        if k:
            there = {"expert": flip(z, k)}
            back_out[k, at] = acc.astype(bf16)
            back_c[c] = send(
                back_out.at[k, at], back_in.at[k, at], back_s.at[c], back_r.at[c], there
            )
        else:
            total[at] = acc

    n = len(chunks)
    far, near = list(range(2, n - 1)), [1, n - 1]
    for step in range(n):
        stage_a(step)
        if step == 2:
            stage_b(0)
    for c in far[:1]:
        stage_b(c)
    stage_f(0)
    stage_c(0)
    for c in far[1:] + near:
        stage_b(c)
    for c in far + near:
        stage_f(c)
        stage_c(c)

    for copy in back_c.values():
        copy.wait_recv()
    result = total[...]
    for k in others:
        result = result + back_in[k].astype(f32)
    out_ref[...] = result.astype(out_ref.dtype)
    for copy in pending:
        copy.wait_send()


def dense_device(tokens, expert_ids, route_weights, w_gate_up, w_down):
    rows, feature_cols = tokens.shape
    local, _, wide = w_gate_up.shape
    hidden_units, out_cols = w_down.shape[1:]
    n_e = lax.axis_size("expert")
    first = rows // 32 * 16
    chunks = ((0, 0, rows), (1, 0, first)) + tuple((k, 0, rows) for k in range(n_e - 1, 1, -1))
    chunks += ((1, first, rows - first),)
    parts = len(chunks)
    f32, bf16 = jnp.float32, jnp.bfloat16
    vmem = pl.BlockSpec(memory_space=pltpu.VMEM)
    hbm = pl.BlockSpec(memory_space=pltpu.MemorySpace.HBM)
    dma = pltpu.SemaphoreType.DMA
    return pl.pallas_call(
        functools.partial(dense_kernel, chunks),
        out_shape=jax.ShapeDtypeStruct((rows, out_cols), bf16),
        in_specs=[hbm] * 5,
        out_specs=vmem,
        scratch_shapes=[
            pltpu.VMEM(w_gate_up.shape, bf16),
            pltpu.VMEM(w_down.shape, bf16),
            pltpu.VMEM(expert_ids.shape[::-1], expert_ids.dtype),
            pltpu.VMEM(route_weights.shape[::-1], f32),
            pltpu.VMEM((n_e, rows, feature_cols), bf16),
            pltpu.VMEM((n_e, 8, rows), f32),
            pltpu.VMEM((n_e, 8, rows), f32),
            *[pltpu.VMEM((n_e, rows, wide), bf16)] * 6,
            *[pltpu.VMEM((n_e, rows, wide), f32)] * 2,
            pltpu.VMEM((n_e, local, rows, hidden_units), bf16),
            pltpu.VMEM((n_e, rows, out_cols), bf16),
            pltpu.VMEM((n_e, rows, out_cols), bf16),
            pltpu.VMEM((rows, out_cols), f32),
            dma((3,)),
            *[dma((local,))] * 2,
            *[dma((n_e,))] * 4,
            *[dma((parts,))] * 6,
            *[dma((parts, local))] * 2,
            *[dma((parts,))] * 2,
        ],
        compiler_params=pltpu.CompilerParams(
            collective_id=0, has_side_effects=True, vmem_limit_bytes=60 * 1024 * 1024
        ),
    )(tokens, expert_ids.T, route_weights.T, w_gate_up, w_down)


def per_device(tokens, expert_ids, route_weights, w_gate_up, w_down):
    tok_dev = tokens.shape[0]
    top_k = expert_ids.shape[1]
    local_experts = w_gate_up.shape[0]
    n_expert, n_token = lax.axis_size("expert"), lax.axis_size("token")
    experts = local_experts * n_expert
    capacity = max(2, min(tok_dev, tok_dev * top_k * 5 // (2 * experts)))
    dense = capacity >= tok_dev >= 32 and n_expert >= 2 and n_expert & (n_expert - 1) == 0
    if dense and tok_dev % 16 == 0 and n_token == local_experts == 4:
        return dense_device(tokens, expert_ids, route_weights, w_gate_up, w_down)
    return slot_device(tokens, expert_ids, route_weights, w_gate_up, w_down)


def solution(mesh):
    return jax.shard_map(
        per_device,
        mesh=mesh,
        in_specs=(
            P(("groups", "expert"), "token"),
            P(("groups", "expert"), None),
            P(("groups", "expert"), None),
            P("expert", "token", None),
            P("expert", None, "token"),
        ),
        out_specs=P(("groups", "expert"), "token"),
        check_vma=False,
    )
```

```python
import functools

import jax
import jax.numpy as jnp
from jax import lax
from jax.experimental import pallas as pl
from jax.experimental.pallas import tpu as pltpu
from jax.sharding import PartitionSpec as P

MESH = pl.DeviceIdType.MESH


def rank_slots(flat_ids):
    place = jnp.arange(flat_ids.shape[0], dtype=jnp.int32)
    earlier = (flat_ids[:, None] == flat_ids[None, :]) & (place[None, :] < place[:, None])
    return jnp.sum(earlier.astype(jnp.int32), axis=1)


def gate_up_terms(inputs, w_gate_up):
    return jnp.einsum("erd,edf->ref", inputs, w_gate_up, preferred_element_type=jnp.float32)


def expert_block(inputs, gate_up_w, down_w):
    hidden_units = gate_up_w.shape[2] // 2
    summed = lax.psum_scatter(
        gate_up_terms(inputs, gate_up_w).astype(jnp.bfloat16),
        "token",
        scatter_dimension=0,
        tiled=True,
    ).astype(jnp.float32)
    hidden = (jax.nn.silu(summed[..., :hidden_units]) * summed[..., hidden_units:]).astype(
        jnp.bfloat16
    )
    produced = jnp.einsum(
        "reh,ehd->erd",
        lax.all_gather(hidden, "token", axis=0, tiled=True),
        down_w,
        preferred_element_type=jnp.float32,
    )
    return produced.astype(jnp.bfloat16)


def slot_device(tokens, expert_ids, route_weights, w_gate_up, w_down):
    tok_dev, feature_cols = tokens.shape
    top_k = expert_ids.shape[1]
    local_experts = w_gate_up.shape[0]
    n_expert = lax.axis_size("expert")
    experts = local_experts * n_expert
    capacity = max(2, min(tok_dev, tok_dev * top_k * 5 // (2 * experts)))
    slot_count = n_expert * capacity
    flat_ids = expert_ids.reshape(-1)
    rank_of = rank_slots(flat_ids)
    position = (
        flat_ids % local_experts * slot_count + flat_ids // local_experts * capacity + rank_of
    )
    token_of = jnp.arange(flat_ids.shape[0], dtype=jnp.int32) // top_k
    slot_table = (
        jnp.full((local_experts * slot_count,), tok_dev, jnp.int32).at[position].set(token_of)
    )
    padded = jnp.concatenate([tokens, jnp.zeros((1, feature_cols), tokens.dtype)], axis=0)
    outgoing = jnp.take(padded, slot_table, axis=0).reshape(
        local_experts, n_expert, capacity, feature_cols
    )
    arrived = lax.all_to_all(outgoing, "expert", split_axis=1, concat_axis=1, tiled=True)
    inputs = arrived.reshape(local_experts, slot_count, feature_cols)
    expert_out = expert_block(inputs, w_gate_up, w_down)
    returned = lax.all_to_all(
        expert_out.reshape(local_experts, n_expert, capacity, feature_cols),
        "expert",
        split_axis=1,
        concat_axis=1,
        tiled=True,
    )
    picked = jnp.take(
        returned.reshape(local_experts * slot_count, feature_cols), position, axis=0
    ).reshape(tok_dev, top_k, feature_cols)
    combined = jnp.sum(route_weights[:, :, None] * picked.astype(jnp.float32), axis=1)
    return combined.astype(jnp.bfloat16)


def flip(index, bits):
    out, bit = index, 1
    while bit <= bits:
        if bits & bit:
            out = out + bit * (1 - 2 * ((index // bit) % 2))
        bit *= 2
    return out


def dense_kernel(
    chunks,
    tokens_ref,
    ids_hbm,
    weights_hbm,
    wg_hbm,
    wd_hbm,
    out_ref,
    wg,
    wd,
    ids_ref,
    weights_ref,
    tok,
    row_out,
    row_in,
    far_out,
    far_in,
    sum_out,
    sum_in,
    near_out,
    near_in,
    part,
    own,
    hid,
    back_out,
    back_in,
    total,
    load_sem,
    wg_sem,
    wd_sem,
    tok_s,
    tok_r,
    row_s,
    row_r,
    far_s,
    far_r,
    sum_s,
    sum_r,
    near_s,
    near_r,
    hid_s,
    hid_r,
    back_s,
    back_r,
):
    z = lax.axis_index("expert")
    t = lax.axis_index("token")
    rows = tokens_ref.shape[0]
    half = own.shape[2] // 2
    local = wg.shape[0]
    f32, bf16 = jnp.float32, jnp.bfloat16
    mate, across = {"token": flip(t, 1)}, {"token": flip(t, 2)}
    others = []
    for k, _, _ in chunks:
        if k and k not in others:
            others.append(k)

    barrier = pltpu.get_barrier_semaphore()
    partners = [mate, across] + [{"expert": flip(z, k)} for k in others]
    for partner in reversed(partners):
        pl.semaphore_signal(barrier, inc=1, device_id=partner, device_id_type=MESH)

    loads = [
        pltpu.make_async_copy(tokens_ref, tok.at[0], load_sem.at[0]),
        pltpu.make_async_copy(ids_hbm, ids_ref, load_sem.at[1]),
        pltpu.make_async_copy(weights_hbm, weights_ref, load_sem.at[2]),
    ]
    wg_copies, wd_copies = {}, {}
    for j in (3, 2, 1, 0):
        wg_copies[j] = pltpu.make_async_copy(wg_hbm.at[flip(t, j)], wg.at[j], wg_sem.at[j])
    for load in loads:
        load.start()
    for j in (3, 2):
        wg_copies[j].start()
    for load in loads:
        load.wait()

    for k in [0] + others:
        expert = flip(z, k) * local + t
        row = jnp.sum(
            jnp.where(ids_ref[...] == expert, weights_ref[...], 0.0), axis=0, keepdims=True
        )
        row_out[k] = jnp.broadcast_to(row, row_out.shape[1:])

    pending = []

    def send(src, dst, s_sem, r_sem, device):
        copy = pltpu.make_async_remote_copy(
            src_ref=src,
            dst_ref=dst,
            send_sem=s_sem,
            recv_sem=r_sem,
            device_id=device,
            device_id_type=MESH,
        )
        copy.start()
        pending.append(copy)
        return copy

    tok_c, row_c, far_c, sum_c, near_c, back_c, hid_c = {}, {}, {}, {}, {}, {}, {}

    def terms(c, j):
        k, start, size = chunks[c]
        return jnp.dot(tok[k, pl.ds(start, size), :], wg[j], preferred_element_type=f32)

    def piece(c):
        k, start, size = chunks[c]
        return (k, pl.ds(start, size))

    def far_sum(c):
        here = piece(c)
        far_c[c].wait_recv()
        sum_out[here] = (part[here] + far_in[here].astype(f32)).astype(bf16)
        sum_c[c] = send(sum_out.at[here], sum_in.at[here], sum_s.at[c], sum_r.at[c], across)

    def send_far(c):
        here = piece(c)
        far_c[c] = send(far_out.at[here], far_in.at[here], far_s.at[c], far_r.at[c], mate)

    def send_near(c):
        here = piece(c)
        near_c[c] = send(near_out.at[here], near_in.at[here], near_s.at[c], near_r.at[c], mate)

    def send_tokens(some):
        for o in some:
            there = {"expert": flip(z, o)}
            tok_c[o] = send(tokens_ref, tok.at[o], tok_s.at[o], tok_r.at[o], there)

    def first_block():
        here = piece(0)
        for j in (1, 0):
            wg_copies[j].start()
        for j in range(local):
            wd_copies[j] = pltpu.make_async_copy(wd_hbm.at[flip(t, j)], wd.at[j], wd_sem.at[j])
            wd_copies[j].start()
        wg_copies[3].wait()
        far_out[here] = terms(0, 3).astype(bf16)
        wg_copies[2].wait()
        part[here] = terms(0, 2)
        wg_copies[1].wait()
        near_out[here] = terms(0, 1).astype(bf16)
        pl.semaphore_wait(barrier, len(partners))
        send_far(0)
        send_tokens(others[:1])
        send_near(0)
        wg_copies[0].wait()
        own[here] = terms(0, 0)
        far_sum(0)
        send_tokens(others[1:])
        for o in others:
            there = {"expert": flip(z, o)}
            row_c[o] = send(row_out.at[o], row_in.at[o], row_s.at[o], row_r.at[o], there)

    def stage_a(c):
        here = piece(c)
        tok_c[chunks[c][0]].wait_recv()
        far_out[here] = terms(c, 3).astype(bf16)
        send_far(c)
        part[here] = terms(c, 2)
        near_out[here] = terms(c, 1).astype(bf16)
        send_near(c)
        far_sum(c)
        own[here] = terms(c, 0)

    def send_hidden(k, start, size, j, device):
        at, i = pl.ds(start, size), (k, start // size)
        src = hid.at[k, 2 if j == 3 else 0, at]
        hid_c[k, start, j] = send(src, hid.at[k, j, at], hid_s.at[*i, j], hid_r.at[*i, j], device)

    def stage_b(c):
        k, start, size = chunks[c]
        here = piece(c)
        near_c[c].wait_recv()
        if k:
            row_c[k].wait_recv()
        row = row_in[k, :1, :] if k else row_out[k, :1, :]
        eye = start + lax.broadcasted_iota(
            jnp.int32, (size, rows), 0
        ) == lax.broadcasted_iota(jnp.int32, (size, rows), 1)
        column = jnp.sum(jnp.where(eye, row, 0.0), axis=1, keepdims=True)
        sum_c[c].wait_recv()
        gate_up = own[here] + near_in[here].astype(f32) + sum_in[here].astype(f32)
        gate, up = gate_up[:, :half], gate_up[:, half:]
        at = pl.ds(start, size)
        hid[k, 0, at] = (gate / (1.0 + jnp.exp(-gate)) * up * column).astype(bf16)
        if k:
            send_hidden(k, start, size, 2, across)
        send_hidden(k, start, size, 1, mate)

    def down(k, at, j):
        return jnp.dot(hid[k, j, at], wd[j], preferred_element_type=f32)

    def stage_c(c):
        k, start, size = chunks[c]
        at = pl.ds(start, size)
        hid_c[k, start, 1].wait_recv()
        acc = down(k, at, 0) + down(k, at, 1)
        hid_c[k, start, 2].wait_recv()
        send_hidden(k, start, size, 3, mate)
        acc = acc + down(k, at, 2)
        hid_c[k, start, 3].wait_recv()
        back_out[k, at] = (acc + down(k, at, 3)).astype(bf16)
        there = {"expert": flip(z, k)}
        back_c[k] = send(
            back_out.at[k, at], back_in.at[k, at], back_s.at[c], back_r.at[c], there
        )

    halves = [(0, rows // 2), (rows // 2, rows // 2)]

    late = list(range(2, len(chunks))) + [1]
    first_block()
    for c in range(1, len(chunks)):
        stage_a(c)
    for c in [0] + late:
        stage_b(c)
    for start, size in halves:
        send_hidden(0, start, size, 2, across)
    for j in range(local):
        wd_copies[j].wait()
    for c in late:
        stage_c(c)
    hid_c[0, 0, 1].wait_recv()
    total[...] = down(0, pl.ds(0, rows), 0) + down(0, pl.ds(0, rows), 1)
    for start, size in halves:
        hid_c[0, start, 2].wait_recv()
        send_hidden(0, start, size, 3, mate)
        at = pl.ds(start, size)
        total[at] += down(0, at, 2)
    for start, size in halves:
        hid_c[0, start, 3].wait_recv()
        at = pl.ds(start, size)
        total[at] += down(0, at, 3)

    for copy in back_c.values():
        copy.wait_recv()
    result = total[...]
    for k in others:
        result = result + back_in[k].astype(f32)
    out_ref[...] = result.astype(out_ref.dtype)
    for copy in pending:
        copy.wait_send()


def dense_device(tokens, expert_ids, route_weights, w_gate_up, w_down):
    rows, feature_cols = tokens.shape
    local, _, wide = w_gate_up.shape
    hidden_units, out_cols = w_down.shape[1:]
    n_e = lax.axis_size("expert")
    chunks = ((0, 0, rows), (1, 0, rows)) + tuple((k, 0, rows) for k in range(n_e - 1, 1, -1))
    parts = len(chunks)
    f32, bf16 = jnp.float32, jnp.bfloat16
    vmem = pl.BlockSpec(memory_space=pltpu.VMEM)
    hbm = pl.BlockSpec(memory_space=pltpu.MemorySpace.HBM)
    dma = pltpu.SemaphoreType.DMA
    return pl.pallas_call(
        functools.partial(dense_kernel, chunks),
        out_shape=jax.ShapeDtypeStruct((rows, out_cols), bf16),
        in_specs=[hbm] * 5,
        out_specs=vmem,
        scratch_shapes=[
            pltpu.VMEM(w_gate_up.shape, bf16),
            pltpu.VMEM(w_down.shape, bf16),
            pltpu.VMEM(expert_ids.shape[::-1], expert_ids.dtype),
            pltpu.VMEM(route_weights.shape[::-1], f32),
            pltpu.VMEM((n_e, rows, feature_cols), bf16),
            pltpu.VMEM((n_e, 8, rows), f32),
            pltpu.VMEM((n_e, 8, rows), f32),
            *[pltpu.VMEM((n_e, rows, wide), bf16)] * 6,
            *[pltpu.VMEM((n_e, rows, wide), f32)] * 2,
            pltpu.VMEM((n_e, local, rows, hidden_units), bf16),
            pltpu.VMEM((n_e, rows, out_cols), bf16),
            pltpu.VMEM((n_e, rows, out_cols), bf16),
            pltpu.VMEM((rows, out_cols), f32),
            dma((3,)),
            *[dma((local,))] * 2,
            *[dma((n_e,))] * 4,
            *[dma((parts,))] * 6,
            *[dma((n_e, 2, local))] * 2,
            *[dma((parts,))] * 2,
        ],
        compiler_params=pltpu.CompilerParams(
            collective_id=0, has_side_effects=True, vmem_limit_bytes=60 * 1024 * 1024
        ),
    )(tokens, expert_ids.T, route_weights.T, w_gate_up, w_down)


def per_device(tokens, expert_ids, route_weights, w_gate_up, w_down):
    tok_dev = tokens.shape[0]
    top_k = expert_ids.shape[1]
    local_experts = w_gate_up.shape[0]
    n_expert, n_token = lax.axis_size("expert"), lax.axis_size("token")
    experts = local_experts * n_expert
    capacity = max(2, min(tok_dev, tok_dev * top_k * 5 // (2 * experts)))
    dense = capacity >= tok_dev >= 32 and n_expert >= 2 and n_expert & (n_expert - 1) == 0
    if dense and tok_dev % 32 == 0 and n_token == local_experts == 4:
        return dense_device(tokens, expert_ids, route_weights, w_gate_up, w_down)
    return slot_device(tokens, expert_ids, route_weights, w_gate_up, w_down)


def solution(mesh):
    return jax.shard_map(
        per_device,
        mesh=mesh,
        in_specs=(
            P(("groups", "expert"), "token"),
            P(("groups", "expert"), None),
            P(("groups", "expert"), None),
            P("expert", "token", None),
            P("expert", None, "token"),
        ),
        out_specs=P(("groups", "expert"), "token"),
        check_vma=False,
    )
```

```python
import functools

import jax
import jax.numpy as jnp
from jax import lax
from jax.experimental import pallas as pl
from jax.experimental.pallas import tpu as pltpu
from jax.sharding import PartitionSpec as P

MESH = pl.DeviceIdType.MESH


def rank_slots(flat_ids):
    place = jnp.arange(flat_ids.shape[0], dtype=jnp.int32)
    earlier = (flat_ids[:, None] == flat_ids[None, :]) & (place[None, :] < place[:, None])
    return jnp.sum(earlier.astype(jnp.int32), axis=1)


def gate_up_terms(inputs, w_gate_up):
    return jnp.einsum("erd,edf->ref", inputs, w_gate_up, preferred_element_type=jnp.float32)


def expert_block(inputs, gate_up_w, down_w):
    hidden_units = gate_up_w.shape[2] // 2
    summed = lax.psum_scatter(
        gate_up_terms(inputs, gate_up_w).astype(jnp.bfloat16),
        "token",
        scatter_dimension=0,
        tiled=True,
    ).astype(jnp.float32)
    hidden = (jax.nn.silu(summed[..., :hidden_units]) * summed[..., hidden_units:]).astype(
        jnp.bfloat16
    )
    produced = jnp.einsum(
        "reh,ehd->erd",
        lax.all_gather(hidden, "token", axis=0, tiled=True),
        down_w,
        preferred_element_type=jnp.float32,
    )
    return produced.astype(jnp.bfloat16)


def slot_device(tokens, expert_ids, route_weights, w_gate_up, w_down):
    tok_dev, feature_cols = tokens.shape
    top_k = expert_ids.shape[1]
    local_experts = w_gate_up.shape[0]
    n_expert = lax.axis_size("expert")
    experts = local_experts * n_expert
    capacity = max(2, min(tok_dev, tok_dev * top_k * 5 // (2 * experts)))
    slot_count = n_expert * capacity
    flat_ids = expert_ids.reshape(-1)
    rank_of = rank_slots(flat_ids)
    position = (
        flat_ids % local_experts * slot_count + flat_ids // local_experts * capacity + rank_of
    )
    token_of = jnp.arange(flat_ids.shape[0], dtype=jnp.int32) // top_k
    slot_table = (
        jnp.full((local_experts * slot_count,), tok_dev, jnp.int32).at[position].set(token_of)
    )
    padded = jnp.concatenate([tokens, jnp.zeros((1, feature_cols), tokens.dtype)], axis=0)
    outgoing = jnp.take(padded, slot_table, axis=0).reshape(
        local_experts, n_expert, capacity, feature_cols
    )
    arrived = lax.all_to_all(outgoing, "expert", split_axis=1, concat_axis=1, tiled=True)
    inputs = arrived.reshape(local_experts, slot_count, feature_cols)
    expert_out = expert_block(inputs, w_gate_up, w_down)
    returned = lax.all_to_all(
        expert_out.reshape(local_experts, n_expert, capacity, feature_cols),
        "expert",
        split_axis=1,
        concat_axis=1,
        tiled=True,
    )
    picked = jnp.take(
        returned.reshape(local_experts * slot_count, feature_cols), position, axis=0
    ).reshape(tok_dev, top_k, feature_cols)
    combined = jnp.sum(route_weights[:, :, None] * picked.astype(jnp.float32), axis=1)
    return combined.astype(jnp.bfloat16)


def flip(index, bits):
    out, bit = index, 1
    while bit <= bits:
        if bits & bit:
            out = out + bit * (1 - 2 * ((index // bit) % 2))
        bit *= 2
    return out


def dense_kernel(
    chunks,
    tokens_ref,
    ids_hbm,
    weights_hbm,
    wg_hbm,
    wd_hbm,
    out_ref,
    wg,
    wd,
    ids_ref,
    weights_ref,
    tok,
    far_out,
    far_in,
    sum_out,
    sum_in,
    near_out,
    near_in,
    part,
    own,
    hid,
    back_out,
    back_in,
    total,
    load_sem,
    wg_sem,
    wd_sem,
    tok_s,
    tok_r,
    far_s,
    far_r,
    sum_s,
    sum_r,
    near_s,
    near_r,
    hid_s,
    hid_r,
    back_s,
    back_r,
):
    z = lax.axis_index("expert")
    t = lax.axis_index("token")
    rows = tokens_ref.shape[0]
    half = own.shape[2] // 2
    local = wg.shape[0]
    f32, bf16 = jnp.float32, jnp.bfloat16
    mate, across = {"token": flip(t, 1)}, {"token": flip(t, 2)}
    near_z, mid_z = {"expert": flip(z, 1)}, {"expert": flip(z, 3)}
    middle = (z + 1) // 2 % 2
    features = tokens_ref.shape[1]

    barrier = pltpu.get_barrier_semaphore()
    for partner in (near_z, across, mate):
        pl.semaphore_signal(barrier, inc=1, device_id=partner, device_id_type=MESH)

    @pl.when(middle == 1)
    def _():
        pl.semaphore_signal(barrier, inc=1, device_id=mid_z, device_id_type=MESH)

    loads = [
        pltpu.make_async_copy(tokens_ref, tok.at[0, :, pl.ds(0, features)], load_sem.at[0]),
        pltpu.make_async_copy(ids_hbm, ids_ref, load_sem.at[1]),
        pltpu.make_async_copy(weights_hbm, weights_ref, load_sem.at[2]),
    ]
    wg_copies, wd_copies = {}, {}
    for j in (3, 2, 1, 0):
        wg_copies[j] = pltpu.make_async_copy(wg_hbm.at[flip(t, j)], wg.at[j], wg_sem.at[j])
    loads[0].start()
    for j in (3, 2):
        wg_copies[j].start()
    for load in loads[1:]:
        load.start()

    experts = local * lax.axis_size("expert")
    lanes = tok.shape[2] - features

    def list_weights():
        number = lax.broadcasted_iota(jnp.int32, (experts, rows), 0)
        dense = jnp.zeros((experts, rows), f32)
        for k in range(ids_ref.shape[0]):
            dense += jnp.where(ids_ref[k : k + 1, :] == number, weights_ref[k : k + 1, :], 0.0)
        high = dense.astype(bf16)
        low = dense - high.astype(f32)
        spare = jnp.zeros((lanes - 2 * experts, rows), f32)
        packed = jnp.concatenate([high.astype(f32), low, spare], axis=0).astype(bf16)
        eye = lax.broadcasted_iota(jnp.int32, (rows, rows), 0) == lax.broadcasted_iota(
            jnp.int32, (rows, rows), 1
        )
        tok[0, :, pl.ds(features, lanes)] = lax.dot_general(
            jnp.where(eye, 1.0, 0.0).astype(bf16),
            packed,
            (((1,), (1,)), ((), ())),
            preferred_element_type=f32,
        ).astype(bf16)

    pending = []

    def send(src, dst, s_sem, r_sem, device):
        copy = pltpu.make_async_remote_copy(
            src_ref=src,
            dst_ref=dst,
            send_sem=s_sem,
            recv_sem=r_sem,
            device_id=device,
            device_id_type=MESH,
        )
        copy.start()
        pending.append(copy)
        return copy

    far_c, sum_c, near_c, back_c, hid_c = {}, {}, {}, {}, {}

    def terms(c, j):
        k, start, size = chunks[c]
        return jnp.dot(tok[k, pl.ds(start, size), pl.ds(0, features)], wg[j], preferred_element_type=f32)

    def piece(c):
        k, start, size = chunks[c]
        return (k, pl.ds(start, size))

    def far_sum(c):
        here = piece(c)
        far_c[c].wait_recv()
        sum_out[here] = (part[here] + far_in[here].astype(f32)).astype(bf16)
        sum_c[c] = send(sum_out.at[here], sum_in.at[here], sum_s.at[c], sum_r.at[c], across)

    def send_far(c):
        here = piece(c)
        far_c[c] = send(far_out.at[here], far_in.at[here], far_s.at[c], far_r.at[c], mate)

    def send_near(c):
        here = piece(c)
        near_c[c] = send(near_out.at[here], near_in.at[here], near_s.at[c], near_r.at[c], mate)

    hops = ((0, 1, near_z), (0, 3, mid_z), (1, 2, mid_z), (3, 2, near_z), (2, 3, near_z))

    def hop(i):
        src, dst, device = hops[i]
        return pltpu.make_async_remote_copy(
            src_ref=tok.at[src],
            dst_ref=tok.at[dst],
            send_sem=tok_s.at[i],
            recv_sem=tok_r.at[dst],
            device_id=device,
            device_id_type=MESH,
        )

    def forward(i):
        @pl.when(middle == 1)
        def _():
            if i == 3:
                hop(1).wait_recv()
            hop(i).start()

    def tokens_in(c):
        if c == 3:

            @pl.when(middle == 0)
            def _():
                hop(4).wait_recv()
        else:
            hop((0, 2)[c - 1]).wait_recv()
        if c < 3:
            for i in ((2, 3), (4,))[c - 1]:
                forward(i)

    def first_block():
        here = piece(0)
        loads[0].wait()
        wg_copies[3].wait()
        for j in (1, 0):
            wg_copies[j].start()
        far_out[here] = terms(0, 3).astype(bf16)
        pl.semaphore_wait(barrier, 3 + middle)
        send_far(0)
        for load in loads[1:]:
            load.wait()
        list_weights()
        hop(0).start()
        forward(1)
        wg_copies[2].wait()
        part[here] = terms(0, 2)
        far_sum(0)
        wg_copies[1].wait()
        near_out[here] = terms(0, 1).astype(bf16)
        send_near(0)
        for j in range(local):
            wd_copies[j] = pltpu.make_async_copy(wd_hbm.at[flip(t, j)], wd.at[j], wd_sem.at[j])
            wd_copies[j].start()
        wg_copies[0].wait()
        own[here] = terms(0, 0)

    def stage_a(c):
        here = piece(c)
        tokens_in(c)
        far_out[here] = terms(c, 3).astype(bf16)
        send_far(c)
        part[here] = terms(c, 2)
        near_out[here] = terms(c, 1).astype(bf16)
        send_near(c)
        far_sum(c)
        own[here] = terms(c, 0)

    def send_hidden(k, start, size, j, device):
        at, i = pl.ds(start, size), (k, start // size)
        src = hid.at[k, 2 if j == 3 else 0, at]
        hid_c[k, start, j] = send(src, hid.at[k, j, at], hid_s.at[*i, j], hid_r.at[*i, j], device)

    def stage_b(c):
        k, start, size = chunks[c]
        here = piece(c)
        near_c[c].wait_recv()
        lane = lax.broadcasted_iota(jnp.int32, (size, lanes), 1)
        mine = (lane == z * local + t) | (lane == experts + z * local + t)
        listed = tok[k, pl.ds(start, size), pl.ds(features, lanes)].astype(f32)
        column = jnp.sum(jnp.where(mine, listed, 0.0), axis=1, keepdims=True)
        sum_c[c].wait_recv()
        gate_up = own[here] + near_in[here].astype(f32) + sum_in[here].astype(f32)
        gate, up = gate_up[:, :half], gate_up[:, half:]
        at = pl.ds(start, size)
        hid[k, 0, at] = (gate / (1.0 + jnp.exp(-gate)) * up * column).astype(bf16)
        if k:
            send_hidden(k, start, size, 2, across)
        send_hidden(k, start, size, 1, mate)

    def down(k, at, j):
        return jnp.dot(hid[k, j, at], wd[j], preferred_element_type=f32)

    def stage_c(c):
        k, start, size = chunks[c]
        at = pl.ds(start, size)
        hid_c[k, start, 1].wait_recv()
        acc = down(k, at, 0) + down(k, at, 1)
        hid_c[k, start, 2].wait_recv()
        send_hidden(k, start, size, 3, mate)
        acc = acc + down(k, at, 2)
        hid_c[k, start, 3].wait_recv()
        back_out[k, at] = (acc + down(k, at, 3)).astype(bf16)
        there = {"expert": flip(z, k)}
        back_c[k] = send(
            back_out.at[k, at], back_in.at[k, at], back_s.at[c], back_r.at[c], there
        )

    halves = [(0, rows // 2), (rows // 2, rows // 2)]

    late = list(range(2, len(chunks))) + [1]
    first_block()
    for c in range(1, len(chunks)):
        stage_a(c)
    for c in [0] + late:
        stage_b(c)
    for start, size in halves:
        send_hidden(0, start, size, 2, across)
    for j in range(local):
        wd_copies[j].wait()
    for c in late:
        stage_c(c)
    hid_c[0, 0, 1].wait_recv()
    total[...] = down(0, pl.ds(0, rows), 0) + down(0, pl.ds(0, rows), 1)
    for start, size in halves:
        hid_c[0, start, 2].wait_recv()
        send_hidden(0, start, size, 3, mate)
        at = pl.ds(start, size)
        total[at] += down(0, at, 2)
    for start, size in halves:
        hid_c[0, start, 3].wait_recv()
        at = pl.ds(start, size)
        total[at] += down(0, at, 3)

    for copy in back_c.values():
        copy.wait_recv()
    result = total[...]
    for k in back_c:
        result = result + back_in[k].astype(f32)
    out_ref[...] = result.astype(out_ref.dtype)
    for copy in pending:
        copy.wait_send()
    hop(0).wait_send()

    @pl.when(middle == 1)
    def _():
        for i in range(1, len(hops)):
            hop(i).wait_send()


def dense_device(tokens, expert_ids, route_weights, w_gate_up, w_down):
    rows, feature_cols = tokens.shape
    local, _, wide = w_gate_up.shape
    hidden_units, out_cols = w_down.shape[1:]
    n_e = lax.axis_size("expert")
    chunks = ((0, 0, rows), (1, 0, rows)) + tuple((k, 0, rows) for k in range(2, n_e))
    parts = len(chunks)
    f32, bf16 = jnp.float32, jnp.bfloat16
    vmem = pl.BlockSpec(memory_space=pltpu.VMEM)
    hbm = pl.BlockSpec(memory_space=pltpu.MemorySpace.HBM)
    dma = pltpu.SemaphoreType.DMA
    return pl.pallas_call(
        functools.partial(dense_kernel, chunks),
        out_shape=pltpu.VMEM((rows, out_cols), bf16),
        in_specs=[hbm] * 5,
        out_specs=vmem,
        scratch_shapes=[
            pltpu.VMEM(w_gate_up.shape, bf16),
            pltpu.VMEM(w_down.shape, bf16),
            pltpu.VMEM(expert_ids.shape[::-1], expert_ids.dtype),
            pltpu.VMEM(route_weights.shape[::-1], f32),
            pltpu.VMEM((n_e, rows, feature_cols + 128), bf16),
            *[pltpu.VMEM((n_e, rows, wide), bf16)] * 6,
            *[pltpu.VMEM((n_e, rows, wide), f32)] * 2,
            pltpu.VMEM((n_e, local, rows, hidden_units), bf16),
            pltpu.VMEM((n_e, rows, out_cols), bf16),
            pltpu.VMEM((n_e, rows, out_cols), bf16),
            pltpu.VMEM((rows, out_cols), f32),
            dma((3,)),
            *[dma((local,))] * 2,
            dma((n_e + 1,)),
            dma((n_e,)),
            *[dma((parts,))] * 6,
            *[dma((n_e, 2, local))] * 2,
            *[dma((parts,))] * 2,
        ],
        compiler_params=pltpu.CompilerParams(
            collective_id=0, has_side_effects=True, vmem_limit_bytes=60 * 1024 * 1024
        ),
    )(tokens, expert_ids.T, route_weights.T, w_gate_up, w_down)


def per_device(tokens, expert_ids, route_weights, w_gate_up, w_down):
    tok_dev = tokens.shape[0]
    top_k = expert_ids.shape[1]
    local_experts = w_gate_up.shape[0]
    n_expert, n_token = lax.axis_size("expert"), lax.axis_size("token")
    experts = local_experts * n_expert
    capacity = max(2, min(tok_dev, tok_dev * top_k * 5 // (2 * experts)))
    dense = capacity >= tok_dev >= 32 and n_expert == 4
    if dense and tok_dev % 32 == 0 and n_token == local_experts == 4:
        return dense_device(tokens, expert_ids, route_weights, w_gate_up, w_down)
    return slot_device(tokens, expert_ids, route_weights, w_gate_up, w_down)


def solution(mesh):
    return jax.shard_map(
        per_device,
        mesh=mesh,
        in_specs=(
            P(("groups", "expert"), "token"),
            P(("groups", "expert"), None),
            P(("groups", "expert"), None),
            P("expert", "token", None),
            P("expert", None, "token"),
        ),
        out_specs=P(("groups", "expert"), "token"),
        check_vma=False,
    )
```

```python
import functools

import jax
import jax.numpy as jnp
from jax import lax
from jax.experimental import pallas as pl
from jax.experimental.pallas import tpu as pltpu
from jax.sharding import PartitionSpec as P

MESH = pl.DeviceIdType.MESH


def rank_slots(flat_ids):
    place = jnp.arange(flat_ids.shape[0], dtype=jnp.int32)
    earlier = (flat_ids[:, None] == flat_ids[None, :]) & (place[None, :] < place[:, None])
    return jnp.sum(earlier.astype(jnp.int32), axis=1)


def gate_up_terms(inputs, w_gate_up):
    return jnp.einsum("erd,edf->ref", inputs, w_gate_up, preferred_element_type=jnp.float32)


def expert_block(inputs, gate_up_w, down_w):
    hidden_units = gate_up_w.shape[2] // 2
    summed = lax.psum_scatter(
        gate_up_terms(inputs, gate_up_w).astype(jnp.bfloat16),
        "token",
        scatter_dimension=0,
        tiled=True,
    ).astype(jnp.float32)
    hidden = (jax.nn.silu(summed[..., :hidden_units]) * summed[..., hidden_units:]).astype(
        jnp.bfloat16
    )
    produced = jnp.einsum(
        "reh,ehd->erd",
        lax.all_gather(hidden, "token", axis=0, tiled=True),
        down_w,
        preferred_element_type=jnp.float32,
    )
    return produced.astype(jnp.bfloat16)


def slot_device(tokens, expert_ids, route_weights, w_gate_up, w_down):
    tok_dev, feature_cols = tokens.shape
    top_k = expert_ids.shape[1]
    local_experts = w_gate_up.shape[0]
    n_expert = lax.axis_size("expert")
    experts = local_experts * n_expert
    capacity = max(2, min(tok_dev, tok_dev * top_k * 5 // (2 * experts)))
    slot_count = n_expert * capacity
    flat_ids = expert_ids.reshape(-1)
    rank_of = rank_slots(flat_ids)
    position = (
        flat_ids % local_experts * slot_count + flat_ids // local_experts * capacity + rank_of
    )
    token_of = jnp.arange(flat_ids.shape[0], dtype=jnp.int32) // top_k
    slot_table = (
        jnp.full((local_experts * slot_count,), tok_dev, jnp.int32).at[position].set(token_of)
    )
    padded = jnp.concatenate([tokens, jnp.zeros((1, feature_cols), tokens.dtype)], axis=0)
    outgoing = jnp.take(padded, slot_table, axis=0).reshape(
        local_experts, n_expert, capacity, feature_cols
    )
    arrived = lax.all_to_all(outgoing, "expert", split_axis=1, concat_axis=1, tiled=True)
    inputs = arrived.reshape(local_experts, slot_count, feature_cols)
    expert_out = expert_block(inputs, w_gate_up, w_down)
    returned = lax.all_to_all(
        expert_out.reshape(local_experts, n_expert, capacity, feature_cols),
        "expert",
        split_axis=1,
        concat_axis=1,
        tiled=True,
    )
    picked = jnp.take(
        returned.reshape(local_experts * slot_count, feature_cols), position, axis=0
    ).reshape(tok_dev, top_k, feature_cols)
    combined = jnp.sum(route_weights[:, :, None] * picked.astype(jnp.float32), axis=1)
    return combined.astype(jnp.bfloat16)


def flip(index, bits):
    out, bit = index, 1
    while bit <= bits:
        if bits & bit:
            out = out + bit * (1 - 2 * ((index // bit) % 2))
        bit *= 2
    return out


def dense_kernel(
    pieces,
    tokens_ref,
    ids_hbm,
    weights_hbm,
    wg_hbm,
    wd_hbm,
    out_ref,
    wg,
    wd,
    ids_ref,
    weights_ref,
    tok,
    listed,
    far_out,
    far_in,
    sum_out,
    sum_in,
    near_out,
    near_in,
    part,
    own,
    hid,
    back_out,
    back_in,
    total,
    load_sem,
    wg_sem,
    wd_sem,
    tok_s,
    tok_r,
    list_s,
    list_r,
    far_s,
    far_r,
    sum_s,
    sum_r,
    near_s,
    near_r,
    hid_s,
    hid_r,
    back_s,
    back_r,
):
    z = lax.axis_index("expert")
    t = lax.axis_index("token")
    rows = tokens_ref.shape[0]
    half = own.shape[2] // 2
    local = wg.shape[0]
    f32, bf16 = jnp.float32, jnp.bfloat16
    mate, across = {"token": flip(t, 1)}, {"token": flip(t, 2)}
    near_z, mid_z = {"expert": flip(z, 1)}, {"expert": flip(z, 3)}
    middle = (z + 1) // 2 % 2

    barrier = pltpu.get_barrier_semaphore()
    for partner in (near_z, across, mate):
        pl.semaphore_signal(barrier, inc=1, device_id=partner, device_id_type=MESH)

    @pl.when(middle == 1)
    def _():
        pl.semaphore_signal(barrier, inc=1, device_id=mid_z, device_id_type=MESH)

    loads = [
        pltpu.make_async_copy(tokens_ref, tok.at[0], load_sem.at[0]),
        pltpu.make_async_copy(ids_hbm, ids_ref, load_sem.at[1]),
        pltpu.make_async_copy(weights_hbm, weights_ref, load_sem.at[2]),
    ]
    wg_copies, wd_copies = {}, {}
    for j in (3, 2, 1, 0):
        wg_copies[j] = pltpu.make_async_copy(wg_hbm.at[flip(t, j)], wg.at[j], wg_sem.at[j])
    loads[0].start()
    for j in (3, 2):
        wg_copies[j].start()
    for load in loads[1:]:
        load.start()

    experts = local * lax.axis_size("expert")
    lanes = listed.shape[2]

    def list_weights():
        number = lax.broadcasted_iota(jnp.int32, (experts, rows), 0)
        dense = jnp.zeros((experts, rows), f32)
        for k in range(ids_ref.shape[0]):
            dense += jnp.where(ids_ref[k : k + 1, :] == number, weights_ref[k : k + 1, :], 0.0)
        high = dense.astype(bf16)
        low = dense - high.astype(f32)
        spare = jnp.zeros((lanes - 2 * experts, rows), f32)
        packed = jnp.concatenate([high.astype(f32), low, spare], axis=0).astype(bf16)
        eye = lax.broadcasted_iota(jnp.int32, (rows, rows), 0) == lax.broadcasted_iota(
            jnp.int32, (rows, rows), 1
        )
        listed[0] = lax.dot_general(
            jnp.where(eye, 1.0, 0.0).astype(bf16),
            packed,
            (((1,), (1,)), ((), ())),
            preferred_element_type=f32,
        ).astype(bf16)

    pending = []

    def send(src, dst, s_sem, r_sem, device):
        copy = pltpu.make_async_remote_copy(
            src_ref=src,
            dst_ref=dst,
            send_sem=s_sem,
            recv_sem=r_sem,
            device_id=device,
            device_id_type=MESH,
        )
        copy.start()
        pending.append(copy)
        return copy

    far_c, sum_c, near_c, back_c, hid_c, list_c = {}, {}, {}, {}, {}, {}

    def terms(c, j):
        return jnp.dot(tok[c], wg[j], preferred_element_type=f32)

    def far_sum(c):
        far_c[c].wait_recv()
        sum_out[c] = (part[c] + far_in[c].astype(f32)).astype(bf16)
        sum_c[c] = send(sum_out.at[c], sum_in.at[c], sum_s.at[c], sum_r.at[c], across)

    def send_far(c):
        far_c[c] = send(far_out.at[c], far_in.at[c], far_s.at[c], far_r.at[c], mate)

    def send_near(c):
        near_c[c] = send(near_out.at[c], near_in.at[c], near_s.at[c], near_r.at[c], mate)

    hops = ((0, 1, near_z), (0, 3, mid_z), (1, 2, mid_z), (3, 2, near_z), (2, 3, near_z))

    def hop(i):
        src, dst, device = hops[i]
        return pltpu.make_async_remote_copy(
            src_ref=tok.at[src] if src else tokens_ref,
            dst_ref=tok.at[dst],
            send_sem=tok_s.at[i],
            recv_sem=tok_r.at[dst],
            device_id=device,
            device_id_type=MESH,
        )

    def send_lists():
        for k in range(1, listed.shape[0]):
            there = {"expert": flip(z, k)}
            list_c[k] = send(listed.at[0], listed.at[k], list_s.at[k], list_r.at[k], there)

    def forward(i):
        @pl.when(middle == 1)
        def _():
            if i == 3:
                hop(1).wait_recv()
            hop(i).start()

    def tokens_in(k):
        if k == 3:

            @pl.when(middle == 0)
            def _():
                hop(4).wait_recv()
        else:
            hop((0, 2)[k - 1]).wait_recv()
        if k < 3:
            for i in ((2, 3), (4,))[k - 1]:
                forward(i)

    def first_block():
        pl.semaphore_wait(barrier, 3 + middle)
        hop(0).start()
        forward(1)
        loads[0].wait()
        wg_copies[3].wait()
        for j in (1, 0):
            wg_copies[j].start()
        far_out[0] = terms(0, 3).astype(bf16)
        send_far(0)
        wg_copies[2].wait()
        part[0] = terms(0, 2)
        far_sum(0)
        wg_copies[1].wait()
        near_out[0] = terms(0, 1).astype(bf16)
        send_near(0)
        for j in range(local):
            wd_copies[j] = pltpu.make_async_copy(wd_hbm.at[flip(t, j)], wd.at[j], wd_sem.at[j])
            wd_copies[j].start()
        wg_copies[0].wait()
        own[0] = terms(0, 0)
        for load in loads[1:]:
            load.wait()
        list_weights()

    def stage_a(c):
        tokens_in(c)
        far_out[c] = terms(c, 3).astype(bf16)
        send_far(c)
        part[c] = terms(c, 2)
        near_out[c] = terms(c, 1).astype(bf16)
        send_near(c)
        far_sum(c)
        own[c] = terms(c, 0)

    def send_hidden(p, src, dst, device):
        k, start, size = pieces[p]
        at = pl.ds(start, size)
        hid_c[p, dst] = send(
            hid.at[k, src, at], hid.at[k, dst, at], hid_s.at[p, dst], hid_r.at[p, dst], device
        )

    def stage_b(c):
        near_c[c].wait_recv()
        lane = lax.broadcasted_iota(jnp.int32, (rows, lanes), 1)
        mine = (lane == z * local + t) | (lane == experts + z * local + t)
        if c:
            list_c[c].wait_recv()
        column = jnp.sum(jnp.where(mine, listed[c].astype(f32), 0.0), axis=1, keepdims=True)
        sum_c[c].wait_recv()
        for p, (k, start, size) in enumerate(pieces):
            if k == c:
                at = pl.ds(start, size)
                gate_up = own[c, at] + near_in[c, at].astype(f32) + sum_in[c, at].astype(f32)
                gate, up = gate_up[:, :half], gate_up[:, half:]
                scale = column[start : start + size]
                hid[c, 0, at] = (gate / (1.0 + jnp.exp(-gate)) * up * scale).astype(bf16)
                if c:
                    send_hidden(p, 0, 2, across)
                send_hidden(p, 0, 1, mate)

    def down(k, j, at):
        return jnp.dot(hid[k, j, at], wd[j], preferred_element_type=f32)

    def begin():
        for j in range(local):
            wd_copies[j].wait()
        for p in range(len(pieces)):
            hid_c[p, 1].wait_recv()
        whole = pl.ds(0, rows)
        for k in range(total.shape[0]):
            total[k] = down(k, 0, whole) + down(k, 1, whole)

    def pass_on(*some):
        for p in some:
            hid_c[p, 2].wait_recv()
            send_hidden(p, 2, 3, mate)

    def finish(*some):
        for p in some:
            k, start, size = pieces[p]
            at = pl.ds(start, size)
            acc = total[k, at] + down(k, 2, at)
            hid_c[p, 3].wait_recv()
            acc = acc + down(k, 3, at)
            if k == 0:
                total[k, at] = acc
                continue
            back_out[k, at] = acc.astype(bf16)
            there = {"expert": flip(z, k)}
            back_c[p] = send(
                back_out.at[k, at], back_in.at[k, at], back_s.at[p], back_r.at[p], there
            )

    def settle():
        while pending:
            pending.pop().wait_send()

    first_block()
    for k in range(1, total.shape[0]):
        stage_a(k)
    send_lists()
    stage_b(0)
    stage_b(2)
    stage_b(3)
    early, pending[:] = pending[:], []
    stage_b(1)
    for p in (0, 1):
        send_hidden(p, 0, 2, across)
    begin()
    late, pending[:] = pending[:], early
    settle()
    pending[:] = late
    pass_on(4)
    pass_on(5)
    finish(4)
    pass_on(6)
    finish(5)
    pass_on(2)
    finish(6)
    pass_on(3)
    finish(2)
    pass_on(0)
    finish(3)
    pass_on(1)
    late, pending[:] = pending[:], []
    finish(0, 1)
    pending[:] = late
    settle()

    for copy in back_c.values():
        copy.wait_recv()
    result = total[0]
    for k in range(1, total.shape[0]):
        result = result + back_in[k].astype(f32)
    out_ref[...] = result.astype(out_ref.dtype)
    hop(0).wait_send()

    @pl.when(middle == 1)
    def _():
        for i in range(1, len(hops)):
            hop(i).wait_send()


def dense_device(tokens, expert_ids, route_weights, w_gate_up, w_down):
    rows, feature_cols = tokens.shape
    local, _, wide = w_gate_up.shape
    hidden_units, out_cols = w_down.shape[1:]
    n_e = lax.axis_size("expert")
    half = rows // 2
    halves = ((0, half), (half, rows - half))
    pieces = tuple((k, *part) for k in (0, 1) for part in halves) + ((2, 0, rows),)
    pieces += tuple((3, *part) for part in halves)
    parts = len(pieces)
    f32, bf16 = jnp.float32, jnp.bfloat16
    vmem = pl.BlockSpec(memory_space=pltpu.VMEM)
    hbm = pl.BlockSpec(memory_space=pltpu.MemorySpace.HBM)
    dma = pltpu.SemaphoreType.DMA
    return pl.pallas_call(
        functools.partial(dense_kernel, pieces),
        out_shape=pltpu.VMEM((rows, out_cols), bf16),
        in_specs=[hbm] * 5,
        out_specs=vmem,
        scratch_shapes=[
            pltpu.VMEM(w_gate_up.shape, bf16),
            pltpu.VMEM(w_down.shape, bf16),
            pltpu.VMEM(expert_ids.shape[::-1], expert_ids.dtype),
            pltpu.VMEM(route_weights.shape[::-1], f32),
            pltpu.VMEM((n_e, rows, feature_cols), bf16),
            pltpu.VMEM((n_e, rows, 128), bf16),
            *[pltpu.VMEM((n_e, rows, wide), bf16)] * 6,
            *[pltpu.VMEM((n_e, rows, wide), f32)] * 2,
            pltpu.VMEM((n_e, local, rows, hidden_units), bf16),
            pltpu.VMEM((n_e, rows, out_cols), bf16),
            pltpu.VMEM((n_e, rows, out_cols), bf16),
            pltpu.VMEM((n_e, rows, out_cols), f32),
            dma((3,)),
            *[dma((local,))] * 2,
            dma((n_e + 1,)),
            *[dma((n_e,))] * 3,
            *[dma((parts,))] * 6,
            *[dma((parts, local))] * 2,
            *[dma((parts,))] * 2,
        ],
        compiler_params=pltpu.CompilerParams(
            collective_id=0, has_side_effects=True, vmem_limit_bytes=60 * 1024 * 1024
        ),
    )(tokens, expert_ids.T, route_weights.T, w_gate_up, w_down)


def per_device(tokens, expert_ids, route_weights, w_gate_up, w_down):
    tok_dev = tokens.shape[0]
    top_k = expert_ids.shape[1]
    local_experts = w_gate_up.shape[0]
    n_expert, n_token = lax.axis_size("expert"), lax.axis_size("token")
    experts = local_experts * n_expert
    capacity = max(2, min(tok_dev, tok_dev * top_k * 5 // (2 * experts)))
    dense = capacity >= tok_dev >= 32 and n_expert == 4
    if dense and tok_dev % 64 == 0 and n_token == local_experts == 4:
        return dense_device(tokens, expert_ids, route_weights, w_gate_up, w_down)
    return slot_device(tokens, expert_ids, route_weights, w_gate_up, w_down)


def solution(mesh):
    return jax.shard_map(
        per_device,
        mesh=mesh,
        in_specs=(
            P(("groups", "expert"), "token"),
            P(("groups", "expert"), None),
            P(("groups", "expert"), None),
            P("expert", "token", None),
            P("expert", None, "token"),
        ),
        out_specs=P(("groups", "expert"), "token"),
        check_vma=False,
    )
```

```python
import functools

import jax
import jax.numpy as jnp
from jax import lax
from jax.experimental import pallas as pl
from jax.experimental.pallas import tpu as pltpu
from jax.sharding import PartitionSpec as P

MESH = pl.DeviceIdType.MESH


def rank_slots(flat_ids):
    place = jnp.arange(flat_ids.shape[0], dtype=jnp.int32)
    earlier = (flat_ids[:, None] == flat_ids[None, :]) & (place[None, :] < place[:, None])
    return jnp.sum(earlier.astype(jnp.int32), axis=1)


def gate_up_terms(inputs, w_gate_up):
    return jnp.einsum("erd,edf->ref", inputs, w_gate_up, preferred_element_type=jnp.float32)


def expert_block(inputs, gate_up_w, down_w):
    hidden_units = gate_up_w.shape[2] // 2
    summed = lax.psum_scatter(
        gate_up_terms(inputs, gate_up_w).astype(jnp.bfloat16),
        "token",
        scatter_dimension=0,
        tiled=True,
    ).astype(jnp.float32)
    hidden = (jax.nn.silu(summed[..., :hidden_units]) * summed[..., hidden_units:]).astype(
        jnp.bfloat16
    )
    produced = jnp.einsum(
        "reh,ehd->erd",
        lax.all_gather(hidden, "token", axis=0, tiled=True),
        down_w,
        preferred_element_type=jnp.float32,
    )
    return produced.astype(jnp.bfloat16)


def slot_device(tokens, expert_ids, route_weights, w_gate_up, w_down):
    tok_dev, feature_cols = tokens.shape
    top_k = expert_ids.shape[1]
    local_experts = w_gate_up.shape[0]
    n_expert = lax.axis_size("expert")
    experts = local_experts * n_expert
    capacity = max(2, min(tok_dev, tok_dev * top_k * 5 // (2 * experts)))
    slot_count = n_expert * capacity
    flat_ids = expert_ids.reshape(-1)
    rank_of = rank_slots(flat_ids)
    position = (
        flat_ids % local_experts * slot_count + flat_ids // local_experts * capacity + rank_of
    )
    token_of = jnp.arange(flat_ids.shape[0], dtype=jnp.int32) // top_k
    slot_table = (
        jnp.full((local_experts * slot_count,), tok_dev, jnp.int32).at[position].set(token_of)
    )
    padded = jnp.concatenate([tokens, jnp.zeros((1, feature_cols), tokens.dtype)], axis=0)
    outgoing = jnp.take(padded, slot_table, axis=0).reshape(
        local_experts, n_expert, capacity, feature_cols
    )
    arrived = lax.all_to_all(outgoing, "expert", split_axis=1, concat_axis=1, tiled=True)
    inputs = arrived.reshape(local_experts, slot_count, feature_cols)
    expert_out = expert_block(inputs, w_gate_up, w_down)
    returned = lax.all_to_all(
        expert_out.reshape(local_experts, n_expert, capacity, feature_cols),
        "expert",
        split_axis=1,
        concat_axis=1,
        tiled=True,
    )
    picked = jnp.take(
        returned.reshape(local_experts * slot_count, feature_cols), position, axis=0
    ).reshape(tok_dev, top_k, feature_cols)
    combined = jnp.sum(route_weights[:, :, None] * picked.astype(jnp.float32), axis=1)
    return combined.astype(jnp.bfloat16)


def flip(index, bits):
    out, bit = index, 1
    while bit <= bits:
        if bits & bit:
            out = out + bit * (1 - 2 * ((index // bit) % 2))
        bit *= 2
    return out


def dense_kernel(
    blocks,
    pieces,
    tokens_ref,
    ids_hbm,
    weights_hbm,
    wg_hbm,
    wd_hbm,
    out_ref,
    wg,
    wd,
    ids_ref,
    weights_ref,
    tok,
    listed,
    far_out,
    far_in,
    sum_out,
    sum_in,
    near_out,
    near_in,
    part,
    own,
    hid,
    back_out,
    back_in,
    total,
    load_sem,
    wg_sem,
    wd_sem,
    tok_s,
    tok_r,
    list_s,
    list_r,
    far_s,
    far_r,
    sum_s,
    sum_r,
    near_s,
    near_r,
    hid_s,
    hid_r,
    back_s,
    back_r,
):
    z = lax.axis_index("expert")
    t = lax.axis_index("token")
    rows = tokens_ref.shape[0]
    half = own.shape[2] // 2
    local = wg.shape[0]
    f32, bf16 = jnp.float32, jnp.bfloat16
    mate, across = {"token": flip(t, 1)}, {"token": flip(t, 2)}
    near_z, mid_z = {"expert": flip(z, 1)}, {"expert": flip(z, 3)}
    middle = (z + 1) // 2 % 2

    barrier = pltpu.get_barrier_semaphore()
    for partner in (near_z, across, mate):
        pl.semaphore_signal(barrier, inc=1, device_id=partner, device_id_type=MESH)

    @pl.when(middle == 1)
    def _():
        pl.semaphore_signal(barrier, inc=1, device_id=mid_z, device_id_type=MESH)

    loads = [
        pltpu.make_async_copy(tokens_ref, tok.at[0], load_sem.at[0]),
        pltpu.make_async_copy(ids_hbm, ids_ref, load_sem.at[1]),
        pltpu.make_async_copy(weights_hbm, weights_ref, load_sem.at[2]),
    ]
    wg_copies, wd_copies = {}, {}
    for j in (3, 2, 1, 0):
        wg_copies[j] = pltpu.make_async_copy(wg_hbm.at[flip(t, j)], wg.at[j], wg_sem.at[j])
    loads[0].start()
    for j in (3, 2):
        wg_copies[j].start()
    for load in loads[1:]:
        load.start()

    experts = local * lax.axis_size("expert")
    lanes = listed.shape[2]

    def list_weights():
        number = lax.broadcasted_iota(jnp.int32, (experts, rows), 0)
        dense = jnp.zeros((experts, rows), f32)
        for k in range(ids_ref.shape[0]):
            dense += jnp.where(ids_ref[k : k + 1, :] == number, weights_ref[k : k + 1, :], 0.0)
        high = dense.astype(bf16)
        low = dense - high.astype(f32)
        spare = jnp.zeros((lanes - 2 * experts, rows), f32)
        packed = jnp.concatenate([high.astype(f32), low, spare], axis=0).astype(bf16)
        eye = lax.broadcasted_iota(jnp.int32, (rows, rows), 0) == lax.broadcasted_iota(
            jnp.int32, (rows, rows), 1
        )
        listed[0] = lax.dot_general(
            jnp.where(eye, 1.0, 0.0).astype(bf16),
            packed,
            (((1,), (1,)), ((), ())),
            preferred_element_type=f32,
        ).astype(bf16)

    pending = []

    def send(src, dst, s_sem, r_sem, device):
        copy = pltpu.make_async_remote_copy(
            src_ref=src,
            dst_ref=dst,
            send_sem=s_sem,
            recv_sem=r_sem,
            device_id=device,
            device_id_type=MESH,
        )
        copy.start()
        pending.append(copy)
        return copy

    far_c, sum_c, near_c, back_c, hid_c, list_c = {}, {}, {}, {}, {}, {}

    def span(b):
        k, start, size = blocks[b]
        return (k, pl.ds(start, size))

    def terms(b, j):
        return jnp.dot(tok[span(b)], wg[j], preferred_element_type=f32)

    def far_sum(b):
        at = span(b)
        far_c[b].wait_recv()
        sum_out[at] = (part[at] + far_in[at].astype(f32)).astype(bf16)
        sum_c[b] = send(sum_out.at[at], sum_in.at[at], sum_s.at[b], sum_r.at[b], across)

    def send_far(b):
        at = span(b)
        far_c[b] = send(far_out.at[at], far_in.at[at], far_s.at[b], far_r.at[b], mate)

    def send_near(b):
        at = span(b)
        near_c[b] = send(near_out.at[at], near_in.at[at], near_s.at[b], near_r.at[b], mate)

    hops = ((0, 1, near_z), (0, 3, mid_z), (1, 2, mid_z), (3, 2, near_z), (2, 3, near_z), (0, 1, near_z))

    def hop(i):
        src, dst, device = hops[i]
        at = {0: pl.ds(0, rows // 2), 5: pl.ds(rows // 2, rows // 2)}.get(i, pl.ds(0, rows))
        return pltpu.make_async_remote_copy(
            src_ref=tok.at[src, at] if src else tokens_ref.at[at],
            dst_ref=tok.at[dst, at],
            send_sem=tok_s.at[i],
            recv_sem=tok_r.at[dst if i < 5 else 0],
            device_id=device,
            device_id_type=MESH,
        )

    def send_lists():
        for k in range(1, listed.shape[0]):
            there = {"expert": flip(z, k)}
            list_c[k] = send(listed.at[0], listed.at[k], list_s.at[k], list_r.at[k], there)

    def forward(i):
        @pl.when(middle == 1)
        def _():
            if i == 3:
                hop(1).wait_recv()
            hop(i).start()

    def tokens_in(k):
        if k == 3:

            @pl.when(middle == 0)
            def _():
                hop(4).wait_recv()
        else:
            hop((5, 2)[k - 1]).wait_recv()
        if k < 3:
            for i in ((2, 3), (4,))[k - 1]:
                forward(i)

    def first_block():
        pl.semaphore_wait(barrier, 3 + middle)
        hop(0).start()
        hop(5).start()
        forward(1)
        loads[0].wait()
        wg_copies[3].wait()
        for j in (1, 0):
            wg_copies[j].start()
        far_out[span(0)] = terms(0, 3).astype(bf16)
        send_far(0)
        wg_copies[2].wait()
        part[span(0)] = terms(0, 2)
        far_sum(0)
        wg_copies[1].wait()
        near_out[span(0)] = terms(0, 1).astype(bf16)
        send_near(0)
        for j in range(local):
            wd_copies[j] = pltpu.make_async_copy(wd_hbm.at[flip(t, j)], wd.at[j], wd_sem.at[j])
            wd_copies[j].start()
        wg_copies[0].wait()
        own[span(0)] = terms(0, 0)

    def near_block():
        ends = (pl.ds(0, rows // 2), pl.ds(rows // 2, rows // 2))
        for i, at in enumerate(ends):
            if i == 0:
                hop(0).wait_recv()
            else:
                tokens_in(1)
            far_out[1, at] = jnp.dot(tok[1, at], wg[3], preferred_element_type=f32).astype(bf16)
            there = far_in.at[1, at]
            n = 1 + 4 * i
            far_c[n] = send(far_out.at[1, at], there, far_s.at[n], far_r.at[n], mate)
        part[1] = terms(1, 2)
        for i, at in enumerate(ends):
            n = 1 + 4 * i
            far_c[n].wait_recv()
            sum_out[1, at] = (part[1, at] + far_in[1, at].astype(f32)).astype(bf16)
            there = sum_in.at[1, at]
            sum_c[n] = send(sum_out.at[1, at], there, sum_s.at[n], sum_r.at[n], across)
        near_out[1] = terms(1, 1).astype(bf16)
        send_near(1)
        own[1] = terms(1, 0)

    def stage_a(b):
        k, _, _ = blocks[b]
        if k:
            tokens_in(k)
        far_out[span(b)] = terms(b, 3).astype(bf16)
        send_far(b)
        part[span(b)] = terms(b, 2)
        near_out[span(b)] = terms(b, 1).astype(bf16)
        send_near(b)
        if k:
            far_sum(b)
        own[span(b)] = terms(b, 0)

    def send_hidden(p, src, dst, device):
        k, start, size = pieces[p]
        at = pl.ds(start, size)
        hid_c[p, dst] = send(
            hid.at[k, src, at], hid.at[k, dst, at], hid_s.at[p, dst], hid_r.at[p, dst], device
        )

    def stage_b(b):
        c, first, count = blocks[b]
        near_c[b].wait_recv()
        lane = lax.broadcasted_iota(jnp.int32, (count, lanes), 1)
        mine = (lane == z * local + t) | (lane == experts + z * local + t)
        if c and first == 0:
            list_c[c].wait_recv()
        column = jnp.sum(jnp.where(mine, listed[span(b)].astype(f32), 0.0), axis=1, keepdims=True)
        sum_c[b].wait_recv()
        if b == 1:
            sum_c[5].wait_recv()
        for p, (k, start, size) in enumerate(pieces):
            if k == c and first <= start < first + count:
                at = pl.ds(start, size)
                gate_up = own[c, at] + near_in[c, at].astype(f32) + sum_in[c, at].astype(f32)
                gate, up = gate_up[:, :half], gate_up[:, half:]
                scale = column[start - first : start - first + size]
                hid[c, 0, at] = (gate / (1.0 + jnp.exp(-gate)) * up * scale).astype(bf16)
                if c:
                    send_hidden(p, 0, 2, across)
                send_hidden(p, 0, 1, mate)

    def down(k, j, at):
        return jnp.dot(hid[k, j, at], wd[j], preferred_element_type=f32)

    def begin(*some):
        for p in some:
            k, start, size = pieces[p]
            at = pl.ds(start, size)
            hid_c[p, 1].wait_recv()
            total[k, at] = down(k, 0, at) + down(k, 1, at)

    def pass_on(*some):
        for p in some:
            hid_c[p, 2].wait_recv()
            send_hidden(p, 2, 3, mate)

    def finish(*some):
        for p in some:
            k, start, size = pieces[p]
            at = pl.ds(start, size)
            acc = total[k, at] + down(k, 2, at)
            hid_c[p, 3].wait_recv()
            acc = acc + down(k, 3, at)
            if k == 0:
                total[k, at] = acc
                continue
            back_out[k, at] = acc.astype(bf16)
            there = {"expert": flip(z, k)}
            back_c[p] = send(
                back_out.at[k, at], back_in.at[k, at], back_s.at[p], back_r.at[p], there
            )

    def settle():
        while pending:
            pending.pop().wait_send()

    first_block()
    near_block()
    for b in (2, 3):
        stage_a(b)
    for load in loads[1:]:
        load.wait()
    list_weights()
    send_lists()
    stage_b(0)
    for j in range(local):
        wd_copies[j].wait()
    begin(0)
    stage_b(2)
    stage_b(3)
    stage_a(4)
    early, pending[:] = pending[:], []
    stage_b(1)
    far_sum(4)
    send_hidden(0, 0, 2, across)
    begin(4, 5, 6, 2, 3)
    late, pending[:] = pending[:], early
    settle()
    pending[:] = late
    hop(0).wait_send()
    hop(5).wait_send()

    @pl.when(middle == 1)
    def _():
        for i in range(1, 5):
            hop(i).wait_send()

    pass_on(4)
    pass_on(5)
    finish(4)
    pass_on(6)
    finish(5)
    pass_on(2)
    finish(6)
    pass_on(3)
    finish(2)
    stage_b(4)
    send_hidden(1, 0, 2, across)
    finish(3)
    begin(1)
    pass_on(0)
    finish(0)
    pass_on(1)
    late, pending[:] = pending[:], []
    finish(1)
    pending[:] = late
    settle()

    for copy in back_c.values():
        copy.wait_recv()
    result = total[0]
    for k in range(1, total.shape[0]):
        result = result + back_in[k].astype(f32)
    out_ref[...] = result.astype(out_ref.dtype)


def dense_device(tokens, expert_ids, route_weights, w_gate_up, w_down):
    rows, feature_cols = tokens.shape
    local, _, wide = w_gate_up.shape
    hidden_units, out_cols = w_down.shape[1:]
    n_e = lax.axis_size("expert")
    half, most = rows // 2, rows // 64 * 48
    blocks = ((0, 0, most), *[(k, 0, rows) for k in range(1, n_e)], (0, most, rows - most))
    halves = ((0, half), (half, rows - half))
    pieces = (blocks[0], blocks[-1], *[(1, *part) for part in halves], (2, 0, rows))
    pieces += tuple((3, *part) for part in halves)
    parts = len(pieces)
    f32, bf16 = jnp.float32, jnp.bfloat16
    vmem = pl.BlockSpec(memory_space=pltpu.VMEM)
    hbm = pl.BlockSpec(memory_space=pltpu.MemorySpace.HBM)
    dma = pltpu.SemaphoreType.DMA
    return pl.pallas_call(
        functools.partial(dense_kernel, blocks, pieces),
        out_shape=pltpu.VMEM((rows, out_cols), bf16),
        in_specs=[hbm] * 5,
        out_specs=vmem,
        scratch_shapes=[
            pltpu.VMEM(w_gate_up.shape, bf16),
            pltpu.VMEM(w_down.shape, bf16),
            pltpu.VMEM(expert_ids.shape[::-1], expert_ids.dtype),
            pltpu.VMEM(route_weights.shape[::-1], f32),
            pltpu.VMEM((n_e, rows, feature_cols), bf16),
            pltpu.VMEM((n_e, rows, 128), bf16),
            *[pltpu.VMEM((n_e, rows, wide), bf16)] * 6,
            *[pltpu.VMEM((n_e, rows, wide), f32)] * 2,
            pltpu.VMEM((n_e, local, rows, hidden_units), bf16),
            pltpu.VMEM((n_e, rows, out_cols), bf16),
            pltpu.VMEM((n_e, rows, out_cols), bf16),
            pltpu.VMEM((n_e, rows, out_cols), f32),
            dma((3,)),
            *[dma((local,))] * 2,
            dma((n_e + 2,)),
            *[dma((n_e,))] * 3,
            *[dma((parts,))] * 6,
            *[dma((parts, local))] * 2,
            *[dma((parts,))] * 2,
        ],
        compiler_params=pltpu.CompilerParams(
            collective_id=0, has_side_effects=True, vmem_limit_bytes=60 * 1024 * 1024
        ),
    )(tokens, expert_ids.T, route_weights.T, w_gate_up, w_down)


def per_device(tokens, expert_ids, route_weights, w_gate_up, w_down):
    tok_dev = tokens.shape[0]
    top_k = expert_ids.shape[1]
    local_experts = w_gate_up.shape[0]
    n_expert, n_token = lax.axis_size("expert"), lax.axis_size("token")
    experts = local_experts * n_expert
    capacity = max(2, min(tok_dev, tok_dev * top_k * 5 // (2 * experts)))
    dense = capacity >= tok_dev >= 32 and n_expert == 4
    if dense and tok_dev % 64 == 0 and n_token == local_experts == 4:
        return dense_device(tokens, expert_ids, route_weights, w_gate_up, w_down)
    return slot_device(tokens, expert_ids, route_weights, w_gate_up, w_down)


def solution(mesh):
    return jax.shard_map(
        per_device,
        mesh=mesh,
        in_specs=(
            P(("groups", "expert"), "token"),
            P(("groups", "expert"), None),
            P(("groups", "expert"), None),
            P("expert", "token", None),
            P("expert", None, "token"),
        ),
        out_specs=P(("groups", "expert"), "token"),
        check_vma=False,
    )
```

```python
import functools

import jax
import jax.numpy as jnp
from jax import lax
from jax.experimental import pallas as pl
from jax.experimental.pallas import tpu as pltpu
from jax.sharding import PartitionSpec as P

MESH = pl.DeviceIdType.MESH


def rank_slots(flat_ids):
    place = jnp.arange(flat_ids.shape[0], dtype=jnp.int32)
    earlier = (flat_ids[:, None] == flat_ids[None, :]) & (place[None, :] < place[:, None])
    return jnp.sum(earlier.astype(jnp.int32), axis=1)


def gate_up_terms(inputs, w_gate_up):
    return jnp.einsum("erd,edf->ref", inputs, w_gate_up, preferred_element_type=jnp.float32)


def expert_block(inputs, gate_up_w, down_w):
    hidden_units = gate_up_w.shape[2] // 2
    summed = lax.psum_scatter(
        gate_up_terms(inputs, gate_up_w).astype(jnp.bfloat16),
        "token",
        scatter_dimension=0,
        tiled=True,
    ).astype(jnp.float32)
    hidden = (jax.nn.silu(summed[..., :hidden_units]) * summed[..., hidden_units:]).astype(
        jnp.bfloat16
    )
    produced = jnp.einsum(
        "reh,ehd->erd",
        lax.all_gather(hidden, "token", axis=0, tiled=True),
        down_w,
        preferred_element_type=jnp.float32,
    )
    return produced.astype(jnp.bfloat16)


def slot_device(tokens, expert_ids, route_weights, w_gate_up, w_down):
    tok_dev, feature_cols = tokens.shape
    top_k = expert_ids.shape[1]
    local_experts = w_gate_up.shape[0]
    n_expert = lax.axis_size("expert")
    experts = local_experts * n_expert
    capacity = max(2, min(tok_dev, tok_dev * top_k * 5 // (2 * experts)))
    slot_count = n_expert * capacity
    flat_ids = expert_ids.reshape(-1)
    rank_of = rank_slots(flat_ids)
    position = (
        flat_ids % local_experts * slot_count + flat_ids // local_experts * capacity + rank_of
    )
    token_of = jnp.arange(flat_ids.shape[0], dtype=jnp.int32) // top_k
    slot_table = (
        jnp.full((local_experts * slot_count,), tok_dev, jnp.int32).at[position].set(token_of)
    )
    padded = jnp.concatenate([tokens, jnp.zeros((1, feature_cols), tokens.dtype)], axis=0)
    outgoing = jnp.take(padded, slot_table, axis=0).reshape(
        local_experts, n_expert, capacity, feature_cols
    )
    arrived = lax.all_to_all(outgoing, "expert", split_axis=1, concat_axis=1, tiled=True)
    inputs = arrived.reshape(local_experts, slot_count, feature_cols)
    expert_out = expert_block(inputs, w_gate_up, w_down)
    returned = lax.all_to_all(
        expert_out.reshape(local_experts, n_expert, capacity, feature_cols),
        "expert",
        split_axis=1,
        concat_axis=1,
        tiled=True,
    )
    picked = jnp.take(
        returned.reshape(local_experts * slot_count, feature_cols), position, axis=0
    ).reshape(tok_dev, top_k, feature_cols)
    combined = jnp.sum(route_weights[:, :, None] * picked.astype(jnp.float32), axis=1)
    return combined.astype(jnp.bfloat16)


def flip(index, bits):
    out, bit = index, 1
    while bit <= bits:
        if bits & bit:
            out = out + bit * (1 - 2 * ((index // bit) % 2))
        bit *= 2
    return out


def dense_kernel(
    blocks,
    pieces,
    tokens_ref,
    ids_hbm,
    weights_hbm,
    wg_hbm,
    wd_hbm,
    out_ref,
    wg,
    wd,
    ids_ref,
    weights_ref,
    tok,
    listed,
    far_out,
    far_in,
    sum_out,
    sum_in,
    near_out,
    near_in,
    part,
    own,
    hid,
    back_out,
    back_in,
    total,
    load_sem,
    wg_sem,
    wd_sem,
    tok_s,
    tok_r,
    list_s,
    list_r,
    far_s,
    far_r,
    sum_s,
    sum_r,
    near_s,
    near_r,
    hid_s,
    hid_r,
    back_s,
    back_r,
):
    z = lax.axis_index("expert")
    t = lax.axis_index("token")
    rows = tokens_ref.shape[0]
    half = own.shape[2] // 2
    local = wg.shape[0]
    f32, bf16 = jnp.float32, jnp.bfloat16
    mate, across = {"token": flip(t, 1)}, {"token": flip(t, 2)}
    near_z, mid_z = {"expert": flip(z, 1)}, {"expert": flip(z, 3)}
    middle = (z + 1) // 2 % 2

    barrier = pltpu.get_barrier_semaphore()
    for partner in (near_z, across, mate):
        pl.semaphore_signal(barrier, inc=1, device_id=partner, device_id_type=MESH)

    @pl.when(middle == 1)
    def _():
        pl.semaphore_signal(barrier, inc=1, device_id=mid_z, device_id_type=MESH)

    loads = [
        pltpu.make_async_copy(tokens_ref, tok.at[0], load_sem.at[0]),
        pltpu.make_async_copy(ids_hbm, ids_ref, load_sem.at[1]),
        pltpu.make_async_copy(weights_hbm, weights_ref, load_sem.at[2]),
    ]
    wg_copies, wd_copies = {}, {}
    for j in (3, 2, 1, 0):
        wg_copies[j] = pltpu.make_async_copy(wg_hbm.at[flip(t, j)], wg.at[j], wg_sem.at[j])
    loads[0].start()
    for j in (3, 2):
        wg_copies[j].start()
    for load in loads[1:]:
        load.start()

    experts = local * lax.axis_size("expert")
    lanes = listed.shape[2]

    def list_weights():
        number = lax.broadcasted_iota(jnp.int32, (experts, rows), 0)
        dense = jnp.zeros((experts, rows), f32)
        for k in range(ids_ref.shape[0]):
            dense += jnp.where(ids_ref[k : k + 1, :] == number, weights_ref[k : k + 1, :], 0.0)
        high = dense.astype(bf16)
        low = dense - high.astype(f32)
        spare = jnp.zeros((lanes - 2 * experts, rows), f32)
        packed = jnp.concatenate([high.astype(f32), low, spare], axis=0).astype(bf16)
        eye = lax.broadcasted_iota(jnp.int32, (rows, rows), 0) == lax.broadcasted_iota(
            jnp.int32, (rows, rows), 1
        )
        listed[0] = lax.dot_general(
            jnp.where(eye, 1.0, 0.0).astype(bf16),
            packed,
            (((1,), (1,)), ((), ())),
            preferred_element_type=f32,
        ).astype(bf16)

    pending = []

    def send(src, dst, s_sem, r_sem, device):
        copy = pltpu.make_async_remote_copy(
            src_ref=src,
            dst_ref=dst,
            send_sem=s_sem,
            recv_sem=r_sem,
            device_id=device,
            device_id_type=MESH,
        )
        copy.start()
        pending.append(copy)
        return copy

    far_c, sum_c, near_c, back_c, hid_c, list_c = {}, {}, {}, {}, {}, {}

    def span(b):
        k, start, size = blocks[b]
        return (k, pl.ds(start, size))

    def terms(b, j):
        return jnp.dot(tok[span(b)], wg[j], preferred_element_type=f32)

    def far_sum(b):
        at = span(b)
        far_c[b].wait_recv()
        sum_out[at] = (part[at] + far_in[at].astype(f32)).astype(bf16)
        sum_c[b] = send(sum_out.at[at], sum_in.at[at], sum_s.at[b], sum_r.at[b], across)

    def send_far(b):
        at = span(b)
        far_c[b] = send(far_out.at[at], far_in.at[at], far_s.at[b], far_r.at[b], mate)

    def send_near(b):
        at = span(b)
        near_c[b] = send(near_out.at[at], near_in.at[at], near_s.at[b], near_r.at[b], mate)

    hops = ((0, 1, near_z), (0, 3, mid_z), (1, 2, mid_z), (3, 2, near_z), (2, 3, near_z), (0, 1, near_z))

    def hop(i):
        src, dst, device = hops[i]
        at = {0: pl.ds(0, rows // 2), 5: pl.ds(rows // 2, rows // 2)}.get(i, pl.ds(0, rows))
        return pltpu.make_async_remote_copy(
            src_ref=tok.at[src, at] if src else tokens_ref.at[at],
            dst_ref=tok.at[dst, at],
            send_sem=tok_s.at[i],
            recv_sem=tok_r.at[dst if i < 5 else 0],
            device_id=device,
            device_id_type=MESH,
        )

    def send_lists():
        for k in range(1, listed.shape[0]):
            there = {"expert": flip(z, k)}
            list_c[k] = send(listed.at[0], listed.at[k], list_s.at[k], list_r.at[k], there)

    def forward(i):
        @pl.when(middle == 1)
        def _():
            if i == 3:
                hop(1).wait_recv()
            hop(i).start()

    def tokens_in(k):
        if k == 3:

            @pl.when(middle == 0)
            def _():
                hop(4).wait_recv()
        else:
            hop((5, 2)[k - 1]).wait_recv()
        if k < 3:
            for i in ((2, 3), (4,))[k - 1]:
                forward(i)

    def first_block():
        pl.semaphore_wait(barrier, 3 + middle)
        hop(0).start()
        hop(5).start()
        forward(1)
        loads[0].wait()
        wg_copies[3].wait()
        for j in (1, 0):
            wg_copies[j].start()
        far_out[span(0)] = terms(0, 3).astype(bf16)
        send_far(0)
        wg_copies[2].wait()
        part[span(0)] = terms(0, 2)
        far_sum(0)
        wg_copies[1].wait()
        near_out[span(0)] = terms(0, 1).astype(bf16)
        send_near(0)
        for j in range(local):
            wd_copies[j] = pltpu.make_async_copy(wd_hbm.at[flip(t, j)], wd.at[j], wd_sem.at[j])
            wd_copies[j].start()
        wg_copies[0].wait()
        own[span(0)] = terms(0, 0)

    def near_block():
        ends = (pl.ds(0, rows // 2), pl.ds(rows // 2, rows // 2))
        for i, at in enumerate(ends):
            if i == 0:
                hop(0).wait_recv()
            else:
                tokens_in(1)
            far_out[1, at] = jnp.dot(tok[1, at], wg[3], preferred_element_type=f32).astype(bf16)
            there = far_in.at[1, at]
            n = 1 + 4 * i
            far_c[n] = send(far_out.at[1, at], there, far_s.at[n], far_r.at[n], mate)
        part[1] = terms(1, 2)
        for i, at in enumerate(ends):
            n = 1 + 4 * i
            far_c[n].wait_recv()
            sum_out[1, at] = (part[1, at] + far_in[1, at].astype(f32)).astype(bf16)
            there = sum_in.at[1, at]
            sum_c[n] = send(sum_out.at[1, at], there, sum_s.at[n], sum_r.at[n], across)
        near_out[1] = terms(1, 1).astype(bf16)
        send_near(1)
        own[1] = terms(1, 0)

    def stage_a(b):
        k, _, _ = blocks[b]
        if k:
            tokens_in(k)
        far_out[span(b)] = terms(b, 3).astype(bf16)
        send_far(b)
        part[span(b)] = terms(b, 2)
        near_out[span(b)] = terms(b, 1).astype(bf16)
        send_near(b)
        if k:
            far_sum(b)
        own[span(b)] = terms(b, 0)

    def send_hidden(p, src, dst, device):
        k, start, size = pieces[p]
        at = pl.ds(start, size)
        hid_c[p, dst] = send(
            hid.at[k, src, at], hid.at[k, dst, at], hid_s.at[p, dst], hid_r.at[p, dst], device
        )

    def stage_b(b):
        c, first, count = blocks[b]
        near_c[b].wait_recv()
        lane = lax.broadcasted_iota(jnp.int32, (count, lanes), 1)
        mine = (lane == z * local + t) | (lane == experts + z * local + t)
        if c and first == 0:
            list_c[c].wait_recv()
        column = jnp.sum(jnp.where(mine, listed[span(b)].astype(f32), 0.0), axis=1, keepdims=True)
        sum_c[b].wait_recv()
        if b == 1:
            sum_c[5].wait_recv()
        for p, (k, start, size) in enumerate(pieces):
            if k == c and first <= start < first + count:
                at = pl.ds(start, size)
                gate_up = own[c, at] + near_in[c, at].astype(f32) + sum_in[c, at].astype(f32)
                gate, up = gate_up[:, :half], gate_up[:, half:]
                scale = column[start - first : start - first + size]
                hid[c, 0, at] = (gate / (1.0 + jnp.exp(-gate)) * up * scale).astype(bf16)
                if c:
                    send_hidden(p, 0, 2, across)
                send_hidden(p, 0, 1, mate)

    def down(k, j, at):
        return jnp.dot(hid[k, j, at], wd[j], preferred_element_type=f32)

    def begin(*some):
        for p in some:
            k, start, size = pieces[p]
            at = pl.ds(start, size)
            hid_c[p, 1].wait_recv()
            total[k, at] = down(k, 0, at) + down(k, 1, at)

    def pass_on(*some):
        for p in some:
            hid_c[p, 2].wait_recv()
            send_hidden(p, 2, 3, mate)

    def finish(*some):
        for p in some:
            k, start, size = pieces[p]
            at = pl.ds(start, size)
            acc = total[k, at] + down(k, 2, at)
            hid_c[p, 3].wait_recv()
            acc = acc + down(k, 3, at)
            if k == 0:
                total[k, at] = acc
                continue
            back_out[k, at] = acc.astype(bf16)
            there = {"expert": flip(z, k)}
            back_c[p] = send(
                back_out.at[k, at], back_in.at[k, at], back_s.at[p], back_r.at[p], there
            )

    def settle():
        while pending:
            pending.pop().wait_send()

    first_block()
    near_block()
    for b in (2, 3):
        stage_a(b)
    for load in loads[1:]:
        load.wait()
    list_weights()
    send_lists()
    stage_b(0)
    for j in range(local):
        wd_copies[j].wait()
    begin(0)
    stage_b(2)
    stage_b(3)
    stage_a(4)
    early, pending[:] = pending[:], []
    stage_b(1)
    far_sum(4)
    send_hidden(0, 0, 2, across)
    begin(4, 5, 6, 2, 3)
    late, pending[:] = pending[:], early
    settle()
    pending[:] = late
    hop(0).wait_send()
    hop(5).wait_send()

    @pl.when(middle == 1)
    def _():
        for i in range(1, 5):
            hop(i).wait_send()

    pass_on(4)
    pass_on(5)
    finish(4)
    pass_on(6)
    finish(5)
    pass_on(2)
    finish(6)
    pass_on(3)
    finish(2)
    finish(3)
    stage_b(4)
    send_hidden(1, 0, 2, across)
    begin(1)
    pass_on(0)
    finish(0)
    pass_on(1)
    late, pending[:] = pending[:], []
    finish(1)
    pending[:] = late
    settle()

    for copy in back_c.values():
        copy.wait_recv()
    result = total[0]
    for k in range(1, total.shape[0]):
        result = result + back_in[k].astype(f32)
    out_ref[...] = result.astype(out_ref.dtype)


def dense_device(tokens, expert_ids, route_weights, w_gate_up, w_down):
    rows, feature_cols = tokens.shape
    local, _, wide = w_gate_up.shape
    hidden_units, out_cols = w_down.shape[1:]
    n_e = lax.axis_size("expert")
    half, most = rows // 2, rows // 64 * 48
    blocks = ((0, 0, most), *[(k, 0, rows) for k in range(1, n_e)], (0, most, rows - most))
    halves = ((0, half), (half, rows - half))
    pieces = (blocks[0], blocks[-1], *[(1, *part) for part in halves], (2, 0, rows))
    pieces += tuple((3, *part) for part in halves)
    parts = len(pieces)
    f32, bf16 = jnp.float32, jnp.bfloat16
    vmem = pl.BlockSpec(memory_space=pltpu.VMEM)
    hbm = pl.BlockSpec(memory_space=pltpu.MemorySpace.HBM)
    dma = pltpu.SemaphoreType.DMA
    return pl.pallas_call(
        functools.partial(dense_kernel, blocks, pieces),
        out_shape=pltpu.VMEM((rows, out_cols), bf16),
        in_specs=[hbm] * 5,
        out_specs=vmem,
        scratch_shapes=[
            pltpu.VMEM(w_gate_up.shape, bf16),
            pltpu.VMEM(w_down.shape, bf16),
            pltpu.VMEM(expert_ids.shape[::-1], expert_ids.dtype),
            pltpu.VMEM(route_weights.shape[::-1], f32),
            pltpu.VMEM((n_e, rows, feature_cols), bf16),
            pltpu.VMEM((n_e, rows, 128), bf16),
            *[pltpu.VMEM((n_e, rows, wide), bf16)] * 6,
            *[pltpu.VMEM((n_e, rows, wide), f32)] * 2,
            pltpu.VMEM((n_e, local, rows, hidden_units), bf16),
            pltpu.VMEM((n_e, rows, out_cols), bf16),
            pltpu.VMEM((n_e, rows, out_cols), bf16),
            pltpu.VMEM((n_e, rows, out_cols), f32),
            dma((3,)),
            *[dma((local,))] * 2,
            dma((n_e + 2,)),
            *[dma((n_e,))] * 3,
            *[dma((parts,))] * 6,
            *[dma((parts, local))] * 2,
            *[dma((parts,))] * 2,
        ],
        compiler_params=pltpu.CompilerParams(
            collective_id=0, has_side_effects=True, vmem_limit_bytes=60 * 1024 * 1024
        ),
    )(tokens, expert_ids.T, route_weights.T, w_gate_up, w_down)


def per_device(tokens, expert_ids, route_weights, w_gate_up, w_down):
    tok_dev = tokens.shape[0]
    top_k = expert_ids.shape[1]
    local_experts = w_gate_up.shape[0]
    n_expert, n_token = lax.axis_size("expert"), lax.axis_size("token")
    experts = local_experts * n_expert
    capacity = max(2, min(tok_dev, tok_dev * top_k * 5 // (2 * experts)))
    dense = capacity >= tok_dev >= 32 and n_expert == 4
    if dense and tok_dev % 64 == 0 and n_token == local_experts == 4:
        return dense_device(tokens, expert_ids, route_weights, w_gate_up, w_down)
    return slot_device(tokens, expert_ids, route_weights, w_gate_up, w_down)


def solution(mesh):
    return jax.shard_map(
        per_device,
        mesh=mesh,
        in_specs=(
            P(("groups", "expert"), "token"),
            P(("groups", "expert"), None),
            P(("groups", "expert"), None),
            P("expert", "token", None),
            P("expert", None, "token"),
        ),
        out_specs=P(("groups", "expert"), "token"),
        check_vma=False,
    )
```
